32 devices in a mesh: groups: 2 (over y), row: 4 (over z), col: 4 (over x, core).
Axes of the slice: x: 2, y: 2, z: 4, core: 2. Of those that a mesh axis runs over, the one named last changes fastest.
Arguments:
- right_side: float32 [4096, 512], P(('groups', 'row')), parts along dimension 0, may hold values from -6 to 6
- prev_factor: float32 [4096, 4096], P(('groups', 'row'), 'col'), parts along dimension 0, may hold values from -0.09375 to 0.09375
- prev_solution: float32 [8192, 512], P(('groups', 'col'), 'row'), parts along dimension 0, may hold values from -6 to 6
- window_factor: float32 [4096, 1536], P(('groups', 'row')), parts along dimension 0, may hold values from -2 to 2
Outputs:
- panel: float32 [4096, 512], P(('groups', 'row'), 'col'), parts along dimension 0
The draws below stay inside these ranges and needn't reach their ends.
There are 2 independent parts, one for each index of `groups`. The reference program is written for one: setup_inputs(seed, part) draws one part's arguments, and reference() takes and returns one part's arrays. A program takes and returns all parts, laid end to end along the dimension named above; each array names one. Nothing has to cross between parts.
All inputs are finite; a program needn't handle non-finite values.
Results may differ from the reference program's by a relative error of at most 0.0001.
Values sent between devices are 32-bit elements; how exact they have to be, the bound alone decides.
No kernel may reach another device: no remote copies, remote signals or barrier semaphores. Data moves between devices by JAX's collectives and lax.ppermute only.
A program may use at most 64 MiB of HBM per device.

```python
import math
import jax
import jax.numpy as jnp
from jax import lax

BK = 256
NRHS = 512
STEPS = 6
RW = 2
WROWS = 8
PREV = 16


def draw_window_factor(key, part):
    rows = WROWS * BK
    cols = STEPS * BK
    key_base = jax.random.fold_in(key, 11)
    key_diag = jax.random.fold_in(key, 12)
    row_pos = jnp.arange(rows)[:, None]
    col_pos = jnp.arange(cols)[None, :]
    storage = row_pos // BK
    elimination = storage % RW * (WROWS // RW) + storage // RW
    column_block = col_pos // BK
    within_row = row_pos % BK
    within_col = col_pos % BK
    base = jax.random.normal(key_base, (rows, cols), jnp.float32)
    offdiag = base * (0.4 / math.sqrt(BK))
    lower_part = jnp.where(within_col < within_row, base * (0.7 / math.sqrt(BK)), 0.0)
    diag_values = jax.random.uniform(key_diag, (rows, cols), jnp.float32, 0.5, 1.5)
    inner = jnp.where(within_col == within_row, diag_values, lower_part)
    return jnp.where(column_block == elimination, inner, offdiag).astype(jnp.float32)


def levels(rng, dims, shards, least, top_value):
    gain, own = 1.0, jax.random.fold_in(rng, 6)
    for axis_at, shards_of in shards:
        draws = jnp.exp(jax.random.uniform(jax.random.fold_in(own, axis_at), (shards_of,), jnp.float32, least / len(shards), top_value / len(shards)))
        gain = gain * jnp.repeat(draws, dims[axis_at] // shards_of).reshape([-1 if axis == axis_at else 1 for axis in range(len(dims))])
    return gain


def scatter_about(own_key, extent, spread, most, split=(), dtype=jnp.bfloat16):
    entries = spread * jax.random.normal(own_key, extent, jnp.float32)
    if split:
        entries = entries * levels(own_key, extent, split, -0.22, 0.18)
    return jnp.clip(entries, -most, most).astype(dtype)


def setup_inputs(seed: int = 0, part: int = 0) -> dict:
    seeds = jax.random.split(jax.random.key(seed), 5)
    part_splits = jax.random.split(jax.random.fold_in(seeds[4], part), 5)
    right_side = scatter_about(part_splits[0], (WROWS * BK, NRHS), 1.0, 6.0, ((0, 4),), jnp.float32)
    prev_factor = scatter_about(part_splits[1], (WROWS * BK, PREV * BK), (PREV * BK) ** -0.5, 0.09375, ((0, 4), (1, 4)), jnp.float32)
    prev_solution = scatter_about(part_splits[2], (PREV * BK, NRHS), 1.0, 6.0, ((0, 4), (1, 4)), jnp.float32)
    window_factor = draw_window_factor(jax.random.fold_in(jax.random.fold_in(seeds[4], part), 71), part)
    return {"right_side": right_side, "prev_factor": prev_factor, "prev_solution": prev_solution, "window_factor": window_factor}


def reference(right_side, prev_factor, prev_solution, window_factor):
    rows_count = WROWS // RW
    prior = jnp.dot(prev_factor, prev_solution, precision=lax.Precision.HIGHEST, preferred_element_type=jnp.float32)
    residual = right_side - prior
    resid = residual.reshape(rows_count, RW, BK, NRHS).transpose(1, 0, 2, 3).reshape(WROWS, BK, NRHS)
    tiles = window_factor.reshape(rows_count, RW, BK, STEPS, BK).transpose(1, 0, 2, 3, 4).reshape(WROWS, BK, STEPS, BK)
    order = jnp.arange(WROWS)
    for step in range(STEPS):
        solved = jnp.dot(tiles[step, :, step, :], resid[step], precision=lax.Precision.HIGHEST, preferred_element_type=jnp.float32)
        update = jnp.einsum("eij,jn->ein", tiles[:, :, step, :], solved, precision=lax.Precision.HIGHEST)
        later = (order > step)[:, None, None]
        resid = jnp.where(later, resid - update, resid)
        resid = jnp.where((order == step)[:, None, None], solved[None], resid)
    panel = resid.reshape(RW, rows_count, BK, NRHS).transpose(1, 0, 2, 3).reshape(WROWS * BK, NRHS)
    return panel
```

```python
import jax
import jax.numpy as jnp
from jax import lax
from jax.sharding import PartitionSpec as P

NRHS = 512
STEPS = 6
HIGH = lax.Precision.HIGH


def mul(a, b):
    return jnp.dot(a, b, precision=HIGH, preferred_element_type=jnp.float32)


def general(right_side, prev_factor, prev_solution, window_factor):
    row_count = lax.axis_size("row")
    row_index = lax.axis_index("row")
    col_count = lax.axis_size("col")
    col_index = lax.axis_index("col")
    blocks = window_factor.shape[1] // STEPS
    slots = right_side.shape[0] // blocks
    width = NRHS // col_count
    partial_value = mul(prev_factor, lax.all_gather(prev_solution, "row", axis=1, tiled=True))
    prior = lax.psum_scatter(partial_value, "col", scatter_dimension=1, tiled=True)
    mine = lax.dynamic_slice_in_dim(right_side, col_index * width, width, 1)
    resid = (mine - prior).reshape(slots, blocks, width)
    tiles = window_factor.reshape(slots, blocks, STEPS, blocks)
    order = jnp.arange(slots, dtype=jnp.int32) * row_count + row_index
    for step in range(STEPS):
        root = step % row_count
        solved = mul(tiles[step // row_count, :, step, :], resid[step // row_count])
        solved = lax.psum(jnp.where(row_index == root, solved, jnp.zeros_like(solved)), "row")
        update = jnp.einsum("sij,jn->sin", tiles[:, :, step, :], solved, precision=HIGH)
        resid = jnp.where((order > step)[:, None, None], resid - update, resid)
        resid = jnp.where((order == step)[:, None, None], solved[None], resid)
    return resid.reshape(slots * blocks, width)


def gather_row(piece, chunks):
    row_index = lax.axis_index("row")
    rows = piece.shape[0] // chunks
    up = down = [piece[i * rows : (i + 1) * rows] for i in range(chunks)]
    ups, downs = [], []
    for hop in range(3):
        up = [lax.ppermute(c, "row", [(i, i + 1) for i in range(hop, 3)]) for c in up]
        down = [lax.ppermute(c, "row", [(i + 1, i) for i in range(0, 3 - hop)]) for c in down]
        ups.append(up)
        downs.append(down)
    got = [piece]
    for s in range(1, 4):
        got.append(
            jnp.concatenate(
                [jnp.where(row_index >= s, u, d) for u, d in zip(ups[s - 1], downs[3 - s])], 0
            )
        )
    return got


def line4(right_side, prev_factor, prev_solution, window_factor):
    row_index = lax.axis_index("row")
    col_index = lax.axis_index("col")
    core, side = col_index % 2, col_index // 2
    blocks = window_factor.shape[1] // STEPS
    width = NRHS // 4
    rows = right_side.shape[0]

    got = gather_row(prev_solution, 2)
    parts = jnp.stack([mul(prev_factor, g) for g in got])

    def part(owner):
        return lax.dynamic_index_in_dim(parts, (row_index - owner) % 4, 0, keepdims=False)

    away = jnp.stack([part(1 - core), part(3 - core)])
    keep = jnp.stack([part(core), part(2 + core)])
    keep = keep + lax.ppermute(away, "col", [(0, 1), (1, 0), (2, 3), (3, 2)])
    other = lax.dynamic_index_in_dim(keep, 1 - side, 0, keepdims=False)
    own = lax.dynamic_index_in_dim(keep, side, 0, keepdims=False)
    prior = own + lax.ppermute(other, "col", [(0, 2), (2, 0), (1, 3), (3, 1)])
    mine = lax.dynamic_slice_in_dim(right_side, col_index * width, width, 1)
    resid = mine - prior

    def tile(slot, step):
        return window_factor[slot * blocks : (slot + 1) * blocks, step * blocks : (step + 1) * blocks]

    low, high = resid[:blocks], resid[blocks:]
    at = {}
    done = {}
    for step in range(STEPS):
        root, slot = step % 4, step // 4
        value = low if slot == 0 else high
        for k in range(step):
            value = value - mul(tile(slot, k), at[k, root])
        solved = mul(tile(slot, step), value)
        done[step] = solved
        for d in [(root + 1) % 4, (root + 2) % 4, (root + 3) % 4]:
            if d + 4 > step:
                at[step, d] = lax.ppermute(solved, "row", [(root, d)])
        at[step, root] = solved
    tails = [high, high]
    for i, d in enumerate((2, 3)):
        for k in range(STEPS):
            tails[i] = tails[i] - mul(tile(1, k), at[k, d])
    low = lax.select_n(row_index, *[done[k] for k in range(4)])
    high = lax.select_n(row_index, done[4], done[5], tails[0], tails[1])
    return jnp.concatenate([low, high], 0)


def body(right_side, prev_factor, prev_solution, window_factor):
    blocks = window_factor.shape[1] // STEPS
    slots = right_side.shape[0] // blocks
    if lax.axis_size("row") == 4 and lax.axis_size("col") == 4 and slots == 2:
        return line4(right_side, prev_factor, prev_solution, window_factor)
    return general(right_side, prev_factor, prev_solution, window_factor)


def solution(mesh):
    in_specs = (
        P(("groups", "row"), None),
        P(("groups", "row"), "col"),
        P(("groups", "col"), "row"),
        P(("groups", "row"), None),
    )
    out_specs = P(("groups", "row"), "col")
    return jax.shard_map(body, mesh=mesh, in_specs=in_specs, out_specs=out_specs, check_vma=False)
```

```python
import jax
import jax.numpy as jnp
from jax import lax
from jax.experimental import pallas as pl
from jax.experimental.pallas import tpu as pltpu
from jax.sharding import PartitionSpec as P

NRHS = 512
STEPS = 6
HIGH = lax.Precision.HIGH


def mul(a, b):
    return jnp.dot(a, b, precision=HIGH, preferred_element_type=jnp.float32)


def general(right_side, prev_factor, prev_solution, window_factor):
    row_count = lax.axis_size("row")
    row_index = lax.axis_index("row")
    col_count = lax.axis_size("col")
    col_index = lax.axis_index("col")
    blocks = window_factor.shape[1] // STEPS
    slots = right_side.shape[0] // blocks
    width = NRHS // col_count
    partial_value = mul(prev_factor, lax.all_gather(prev_solution, "row", axis=1, tiled=True))
    prior = lax.psum_scatter(partial_value, "col", scatter_dimension=1, tiled=True)
    mine = lax.dynamic_slice_in_dim(right_side, col_index * width, width, 1)
    resid = (mine - prior).reshape(slots, blocks, width)
    tiles = window_factor.reshape(slots, blocks, STEPS, blocks)
    order = jnp.arange(slots, dtype=jnp.int32) * row_count + row_index
    for step in range(STEPS):
        root = step % row_count
        solved = mul(tiles[step // row_count, :, step, :], resid[step // row_count])
        solved = lax.psum(jnp.where(row_index == root, solved, jnp.zeros_like(solved)), "row")
        update = jnp.einsum("sij,jn->sin", tiles[:, :, step, :], solved, precision=HIGH)
        resid = jnp.where((order > step)[:, None, None], resid - update, resid)
        resid = jnp.where((order == step)[:, None, None], solved[None], resid)
    return resid.reshape(slots * blocks, width)


def gather_row(piece, chunks):
    rows = piece.shape[0] // chunks
    up = down = [piece[i * rows : (i + 1) * rows] for i in range(chunks)]
    ups, downs = [], []
    for hop in range(3):
        up = [lax.ppermute(c, "row", [(i, i + 1) for i in range(hop, 3)]) for c in up]
        down = [lax.ppermute(c, "row", [(i + 1, i) for i in range(0, 3 - hop)]) for c in down]
        ups.append(up)
        downs.append(down)
    return ups, downs


def pick(pred, ones, others):
    return [jnp.where(pred, a, b) for a, b in zip(ones, others)]


def prior_block(prev_factor, prev_solution):
    row_index = lax.axis_index("row")
    col_index = lax.axis_index("col")
    core, side = col_index % 2, col_index // 2
    ups, downs = gather_row(prev_solution, 2)
    half = prev_solution.shape[0] // 2
    whole = [prev_solution[:half], prev_solution[half:]]
    second = pick(row_index >= 2, ups[1], downs[1])
    front = pick(row_index >= 1, ups[0], downs[2])
    back = pick(row_index >= 3, ups[2], downs[0])
    factor, whole[0], whole[1], second[0], second[1] = lax.optimization_barrier(
        (prev_factor, whole[0], whole[1], second[0], second[1])
    )
    mine_first = row_index // 2 == side
    mine_late = ((row_index + 3) % 4) // 2 == side

    def products(flag, one, two):
        close = jnp.concatenate(pick(flag, one, two), 0)
        far = jnp.concatenate(pick(flag, two, one), 0)
        return mul(factor, close), mul(factor, far)

    early = products(mine_first, whole, second)
    late = products(mine_late, front, back)
    keeps_early = core == row_index % 2
    away = jnp.stack([jnp.where(keeps_early, b, a) for a, b in zip(early, late)])
    keep = jnp.stack([jnp.where(keeps_early, a, b) for a, b in zip(early, late)])
    keep = keep + lax.ppermute(away, "col", [(0, 1), (1, 0), (2, 3), (3, 2)])
    return keep[0], lax.ppermute(keep[1], "col", [(0, 2), (2, 0), (1, 3), (3, 1)]), second[0]


BLOCK = 256
HALF = BLOCK // 2
WIDTH = 128
VMEM_SPEC = pl.BlockSpec(memory_space=pltpu.VMEM)
ANY_SPEC = pl.BlockSpec(memory_space=pl.ANY)


def near(x):
    return pltpu.with_memory_space_constraint(x, pltpu.VMEM)


def after(x, *earlier):
    return lax.optimization_barrier((x, *earlier))[0]


def split(x):
    high = x.astype(jnp.bfloat16)
    return high, (x - high.astype(jnp.float32)).astype(jnp.bfloat16)


def wide(x):
    return jnp.concatenate(split(x), 1)


def product(tile, pair):
    high, low = split(tile)
    both = jnp.dot(high, pair, preferred_element_type=jnp.float32)
    both = both + jnp.dot(low, pair, preferred_element_type=jnp.float32)
    return both[:, :WIDTH] + both[:, WIDTH:]


def columns(k):
    return slice(k * BLOCK, (k + 1) * BLOCK)


LOW, TOP = slice(0, BLOCK), slice(BLOCK, 2 * BLOCK)


def call(kernel, shapes, scratch=(), specs=None):
    def run(*args):
        spaces = specs or [VMEM_SPEC] * len(args)
        args = [a if s is ANY_SPEC else near(a) for a, s in zip(args, spaces)]
        return pl.pallas_call(
            kernel,
            out_shape=[pltpu.VMEM(s, jnp.float32) for s in shapes],
            in_specs=spaces,
            out_specs=[VMEM_SPEC] * len(shapes),
            scratch_shapes=list(scratch),
            compiler_params=pltpu.CompilerParams(vmem_limit_bytes=32 * 1024 * 1024),
        )(*args)

    return run


def load_kernel(factor, side, factor_out, side_out, *rest):
    sent, sem = rest[:-1], rest[-1]
    col_index = lax.axis_index("col")
    low = pl.ds(pl.multiple_of((col_index % 2) * HALF, HALF), HALF)
    top = pl.ds(pl.multiple_of(BLOCK + (col_index % 2) * HALF, HALF), HALF)
    mine = pl.ds(pl.multiple_of(col_index * WIDTH, WIDTH), WIDTH)
    sources = [
        factor,
        side.at[:, mine],
        factor.at[low, pl.ds(0, 4 * BLOCK)],
        factor.at[top, pl.ds(BLOCK, 4 * BLOCK)],
        factor.at[top, pl.ds(2 * BLOCK, 4 * BLOCK)],
        factor.at[top, pl.ds(0, 6 * BLOCK)],
    ]
    copies = [
        pltpu.make_async_copy(s, d, sem.at[i])
        for i, (s, d) in enumerate(zip(sources, (factor_out, side_out, *sent)))
    ]
    for copy in copies:
        copy.start()
    for copy in copies:
        copy.wait()


def first_kernel(side, one, two, factor, low, top):
    low[...] = side[LOW, :] - (one[LOW, :] + two[LOW, :])
    top[...] = side[TOP, :] - (one[TOP, :] + two[TOP, :])

    @pl.when(lax.axis_index("row") == 0)
    def _():
        low[...] = product(factor[LOW, columns(0)], wide(low[...]))
        top[...] = top[...] - product(factor[TOP, columns(0)], wide(low[...]))


def second_kernel(solved, low_in, top_in, factor, low, top):
    @pl.when(lax.axis_index("row") == 1)
    def _():
        pair = wide(solved[...])
        value = low_in[...] - product(factor[LOW, columns(0)], pair)
        low[...] = product(factor[LOW, columns(1)], wide(value))
        value = top_in[...] - product(factor[TOP, columns(0)], pair)
        top[...] = value - product(factor[TOP, columns(1)], wide(low[...]))


def halves():
    core = lax.axis_index("col") % 2
    own = pl.ds(pl.multiple_of(core * HALF, HALF), HALF)
    other = pl.ds(pl.multiple_of((1 - core) * HALF, HALF), HALF)
    return own, other


def third_kernel(solved, low, top, low3, top3, factor, own3, other3, own7, other7, state):
    @pl.when(lax.axis_index("row") == 2)
    def _():
        own, other = halves()
        pair = wide(solved[...])
        state[0] = low[...] - product(factor[LOW, columns(0)], pair)
        state[2] = top[...] - product(factor[TOP, columns(0)], pair)
        state[1] = low3[...]
        state[3] = top3[...]
        for at, mine, theirs in ((1, own3, other3), (3, own7, other7)):
            state[at, own, :] = state[at, own, :] - product(mine[:, columns(0)], pair)
            state[at, other, :] = state[at, other, :] - product(theirs[:, columns(0)], pair)


def fourth_kernel(
    state, solved, value4, value5, factor, own3, other3, own4, other4, own5, other5, own7, other7,
    kept, block4, block5, sent, value,
):
    @pl.when(lax.axis_index("row") == 2)
    def _():
        own, other = halves()
        spots = {3: value.at[0], 4: value.at[1], 5: value.at[2], 7: value.at[3], 6: value.at[4]}
        tiles = {
            3: (own3, other3, 0),
            4: (own4, other4, 1),
            5: (own5, other5, 2),
            7: (own7, other7, 0),
        }

        def update(block, k, pair):
            ref = spots[block]
            if block == 6:
                ref[...] = ref[...] - product(factor[TOP, columns(k)], pair)
                return
            mine, theirs, skip = tiles[block]
            ref[own, :] = ref[own, :] - product(mine[:, columns(k - skip)], pair)
            ref[other, :] = ref[other, :] - product(theirs[:, columns(k - skip)], pair)

        pair = wide(solved[...])
        start = state[0] - product(factor[LOW, columns(1)], pair)
        kept[LOW, :] = product(factor[LOW, columns(2)], wide(start))
        value[0] = state[1]
        value[1] = value4[...]
        value[2] = value5[...]
        value[3] = state[3]
        value[4] = state[2]
        for block in (3, 4, 6, 7):
            update(block, 1, pair)
        outs = {2: kept.at[LOW, :], 3: sent.at[LOW, :], 4: block4, 5: block5}
        for k in range(2, 6):
            if k > 2:
                pair = wide(spots[k][...])
                mine, theirs, skip = tiles[k]
                outs[k][own, :] = product(mine[:, columns(k - skip)], pair)
                outs[k][other, :] = product(theirs[:, columns(k - skip)], pair)
            pair = wide(outs[k][...])
            for block in (3, 4, 5, 6, 7):
                if block > k:
                    update(block, k, pair)
        kept[TOP, :] = spots[6][...]
        sent[TOP, :] = spots[7][...]


def line4(right_side, prev_factor, prev_solution, window_factor):
    row_index = lax.axis_index("row")
    one, two, early = prior_block(prev_factor, prev_solution)

    def move(x, *pairs):
        return lax.ppermute(x, "row", list(pairs))

    def swap(x):
        return lax.ppermute(x, "col", [(0, 1), (1, 0), (2, 3), (3, 2)])

    half, size, six = (HALF, 4 * BLOCK), (BLOCK, WIDTH), (HALF, 6 * BLOCK)
    factor, side, send3, send4, send5, send7 = call(
        load_kernel,
        [window_factor.shape, (2 * BLOCK, WIDTH), half, half, half, six],
        [pltpu.SemaphoreType.DMA((6,))],
        [ANY_SPEC, ANY_SPEC],
    )(after(window_factor, early), right_side)
    own3 = move(send3, (3, 2))
    own5 = move(send5, (1, 2))
    own4 = move(send4, (0, 2))
    own7 = move(send7, (3, 2))

    low, top = call(first_kernel, [size, size])(side, one, two, factor)
    first = move(low, (0, 1), (3, 2))
    second = move(low, (0, 2))
    value4 = move(top, (0, 2))
    top3 = move(top, (3, 2))
    other3, other4, other5, other7 = [swap(after(x, low)) for x in (own3, own4, own5, own7)]
    low1, top1 = call(second_kernel, [size, size])(first, low, top, factor)
    third = move(low1, (1, 2))
    value5 = move(top1, (1, 2))
    (state,) = call(third_kernel, [(4, *size)])(
        after(second, low1), low, top, first, top3, factor, own3, other3, own7, other7
    )
    kept, block4, block5, sent = call(
        fourth_kernel, [(2 * BLOCK, WIDTH), size, size, (2 * BLOCK, WIDTH)], [pltpu.VMEM((5, *size), jnp.float32)]
    )(state, third, value4, value5, factor, own3, other3, own4, other4, own5, other5, own7, other7)
    last = move(sent, (2, 3))
    block5 = move(block5, (2, 1))
    block4 = move(block4, (2, 0))
    lows = lax.select_n(row_index, low, low1, kept[:BLOCK], last[:BLOCK])
    tops = lax.select_n(row_index, block4, block5, kept[BLOCK:], last[BLOCK:])
    return jnp.concatenate([lows, tops], 0)


def body(right_side, prev_factor, prev_solution, window_factor):
    blocks = window_factor.shape[1] // STEPS
    slots = right_side.shape[0] // blocks
    if lax.axis_size("row") == 4 and lax.axis_size("col") == 4 and slots == 2:
        return line4(right_side, prev_factor, prev_solution, window_factor)
    return general(right_side, prev_factor, prev_solution, window_factor)


def solution(mesh):
    in_specs = (
        P(("groups", "row"), None),
        P(("groups", "row"), "col"),
        P(("groups", "col"), "row"),
        P(("groups", "row"), None),
    )
    out_specs = P(("groups", "row"), "col")
    return jax.shard_map(body, mesh=mesh, in_specs=in_specs, out_specs=out_specs, check_vma=False)
```

```python
import jax
import jax.numpy as jnp
from jax import lax
from jax.experimental import pallas as pl
from jax.experimental.pallas import tpu as pltpu
from jax.sharding import PartitionSpec as P

NRHS = 512
STEPS = 6
HIGH = lax.Precision.HIGH


def mul(a, b):
    return jnp.dot(a, b, precision=HIGH, preferred_element_type=jnp.float32)


def general(right_side, prev_factor, prev_solution, window_factor):
    row_count = lax.axis_size("row")
    row_index = lax.axis_index("row")
    col_count = lax.axis_size("col")
    col_index = lax.axis_index("col")
    blocks = window_factor.shape[1] // STEPS
    slots = right_side.shape[0] // blocks
    width = NRHS // col_count
    partial_value = mul(prev_factor, lax.all_gather(prev_solution, "row", axis=1, tiled=True))
    prior = lax.psum_scatter(partial_value, "col", scatter_dimension=1, tiled=True)
    mine = lax.dynamic_slice_in_dim(right_side, col_index * width, width, 1)
    resid = (mine - prior).reshape(slots, blocks, width)
    tiles = window_factor.reshape(slots, blocks, STEPS, blocks)
    order = jnp.arange(slots, dtype=jnp.int32) * row_count + row_index
    for step in range(STEPS):
        root = step % row_count
        solved = mul(tiles[step // row_count, :, step, :], resid[step // row_count])
        solved = lax.psum(jnp.where(row_index == root, solved, jnp.zeros_like(solved)), "row")
        update = jnp.einsum("sij,jn->sin", tiles[:, :, step, :], solved, precision=HIGH)
        resid = jnp.where((order > step)[:, None, None], resid - update, resid)
        resid = jnp.where((order == step)[:, None, None], solved[None], resid)
    return resid.reshape(slots * blocks, width)


def gather_row(piece, chunks, inject, load):
    rows = piece.shape[0] // chunks
    up = down = [piece[i * rows : (i + 1) * rows] for i in range(chunks)]
    ups, downs = [], []
    for hop in range(3):
        if hop == 1:
            up, down = inject(up, down)
            ups[0], downs[0] = up, down
        if hop == 2:
            loaded = load(ups[0][1], downs[0][1])
            up, down = [after(up[0], loaded[0]), up[1]], [after(down[0], loaded[0]), down[1]]
        first = (0, 0, 1)[hop]
        up = [lax.ppermute(c, "row", [(i, i + 1) for i in range(first, 3)]) for c in up]
        last = (3, 3, 1)[hop]
        down = [lax.ppermute(c, "row", [(i + 1, i) for i in range(0, last)]) for c in down]
        ups.append(up)
        downs.append(down)
    return ups, downs, loaded


BLOCK = 256
HALF = BLOCK // 2
WIDTH = 128
VMEM_SPEC = pl.BlockSpec(memory_space=pltpu.VMEM)


def after(x, *earlier):
    return lax.optimization_barrier((x, *earlier))[0]


def split(x):
    high = x.astype(jnp.bfloat16)
    return high, (x - high.astype(jnp.float32)).astype(jnp.bfloat16)


def wide(x):
    return jnp.concatenate(split(x), 1)


def product(tile, pair):
    high, low = split(tile)
    both = jnp.dot(high, pair, preferred_element_type=jnp.float32)
    both = both + jnp.dot(low, pair, preferred_element_type=jnp.float32)
    return both[:, :WIDTH] + both[:, WIDTH:]


def columns(k):
    return slice(k * BLOCK, (k + 1) * BLOCK)


LOW, TOP = slice(0, BLOCK), slice(BLOCK, 2 * BLOCK)


def call(kernel, shapes, scratch=(), space=pltpu.VMEM, inside=True, aliases={}):
    def run(*args):
        return pl.pallas_call(
            kernel,
            out_shape=[(pltpu.VMEM if inside else jax.ShapeDtypeStruct)(s, jnp.float32) for s in shapes],
            in_specs=[pl.BlockSpec(memory_space=space)] * len(args),
            out_specs=[VMEM_SPEC] * len(shapes),
            scratch_shapes=list(scratch),
            input_output_aliases=aliases,
            compiler_params=pltpu.CompilerParams(vmem_limit_bytes=32 * 1024 * 1024),
        )(*[pltpu.with_memory_space_constraint(a, space) for a in args])

    return run


def sent_rows():
    core = lax.axis_index("col") % 2
    low = pl.ds(pl.multiple_of(core * HALF, HALF), HALF)
    return low, pl.ds(pl.multiple_of(BLOCK + core * HALF, HALF), HALF)


def copy_all(pairs, sem):
    copies = [pltpu.make_async_copy(s, d, sem.at[i]) for i, (s, d) in enumerate(pairs)]
    for copy in copies:
        copy.start()
    for copy in copies:
        copy.wait()


def tile_kernel(factor, three_a, three_b, four_a, four_b, sem):
    low, top = sent_rows()
    pairs = []
    for j in range(8):
        out = slice((j % 4) * HALF, (j % 4 + 1) * HALF)
        pairs.append((factor.at[low, pl.ds(j * HALF, HALF)], (three_a, three_b)[j // 4].at[out, :]))
        pairs.append((factor.at[top, pl.ds(BLOCK + j * HALF, HALF)], (four_a, four_b)[j // 4].at[out, :]))
    copy_all(pairs, sem)


def inject_kernel(up_in, down_in, four, three, up, down):
    @pl.when(lax.axis_index("row") == 0)
    def _():
        up[...] = four[...]

    @pl.when(lax.axis_index("row") == 3)
    def _():
        down[...] = three[...]


def load_kernel(past, factor, side, past_out, factor_out, side_out, five, seven, sem):
    _, top = sent_rows()
    mine = pl.ds(pl.multiple_of(lax.axis_index("col") * WIDTH, WIDTH), WIDTH)
    copy_all(
        [
            (past, past_out),
            (factor, factor_out),
            (side.at[:, mine], side_out),
            (factor.at[top, pl.ds(2 * BLOCK, 4 * BLOCK)], five),
            (factor.at[top, pl.ds(0, 6 * BLOCK)], seven),
        ],
        sem,
    )


def pieces(flag, one, two):
    return jnp.concatenate([wide(jnp.where(flag, one, two)), wide(jnp.where(flag, two, one))], 1)


def spread(factor, pair):
    high, low = split(factor)
    both = jnp.dot(high, pair, preferred_element_type=jnp.float32)
    both = both + jnp.dot(low, pair, preferred_element_type=jnp.float32)
    return [both[:, 2 * i * WIDTH : (2 * i + 1) * WIDTH] + both[:, (2 * i + 1) * WIDTH : (2 * i + 2) * WIDTH] for i in range(2)]


def flags():
    row_index = lax.axis_index("row")
    side = lax.axis_index("col") // 2
    return row_index, lax.div(row_index, 2) == side, lax.div(lax.rem(row_index + 3, 4), 2) == side


def late_pair(up1, down3, up3, down1):
    row_index, _, mine_late = flags()
    front = jnp.where(row_index >= 1, up1[...], down3[...])
    back = jnp.where(row_index >= 3, up3[...], down1[...])
    return pieces(mine_late, front, back)


def early_kernel(past, whole, up2a, up2b, down2a, down2b, up1, down3, up3, down1, early, late):
    row_index, mine_first, _ = flags()
    depth = up1.shape[0]
    for at, (u, d) in enumerate(((up2a, down2a), (up2b, down2b))):
        rows = slice(at * depth, (at + 1) * depth)
        pair = pieces(mine_first, whole[rows, :], jnp.where(row_index >= 2, u[...], d[...]))
        got = spread(past[:, rows], pair)
        for i in range(2):
            early[i] = got[i] if at == 0 else early[i] + got[i]
    got = spread(past[:, :depth], late_pair(up1, down3, up3, down1))
    for i in range(2):
        late[i] = got[i]


def late_kernel(past, early, late, up1, down3, up3, down1, away, keep):
    row_index = lax.axis_index("row")
    keeps_early = lax.rem(lax.axis_index("col"), 2) == lax.rem(row_index, 2)
    got = spread(past[:, up1.shape[0] :], late_pair(up1, down3, up3, down1))
    for i in range(2):
        total = late[i] + got[i]
        away[i] = jnp.where(keeps_early, total, early[i])
        keep[i] = jnp.where(keeps_early, early[i], total)


def sum_kernel(keep, came, own, other_low, other_top):
    own[...] = keep[0] + came[0]
    other_low[...] = keep[1, LOW] + came[1, LOW]
    other_top[...] = keep[1, TOP] + came[1, TOP]


def first_kernel(side, one, two, factor, low):
    low[...] = side[LOW, :] - (one[LOW, :] + two[...])

    @pl.when(lax.axis_index("row") == 0)
    def _():
        low[...] = product(factor[LOW, columns(0)], wide(low[...]))


def top_kernel(side, one, two, factor, low, top):
    top[...] = side[TOP, :] - (one[TOP, :] + two[...])

    @pl.when(lax.axis_index("row") == 0)
    def _():
        top[...] = top[...] - product(factor[TOP, columns(0)], wide(low[...]))


def last_kernel(low, low1, kept, last, block4, block5, out):
    row_index = lax.axis_index("row")

    @pl.when(row_index == 0)
    def _():
        out[LOW, :] = low[...]
        out[TOP, :] = block4[...]

    @pl.when(row_index == 1)
    def _():
        out[LOW, :] = low1[...]
        out[TOP, :] = block5[...]

    @pl.when(row_index == 2)
    def _():
        out[...] = kept[...]

    @pl.when(row_index == 3)
    def _():
        out[...] = last[...]


def second_kernel(solved, low_in, top_in, factor, low, top):
    @pl.when(lax.axis_index("row") == 1)
    def _():
        pair = wide(solved[...])
        value = low_in[...] - product(factor[LOW, columns(0)], pair)
        low[...] = product(factor[LOW, columns(1)], wide(value))
        value = top_in[...] - product(factor[TOP, columns(0)], pair)
        top[...] = value - product(factor[TOP, columns(1)], wide(low[...]))


def halves():
    core = lax.axis_index("col") % 2
    own = pl.ds(pl.multiple_of(core * HALF, HALF), HALF)
    other = pl.ds(pl.multiple_of((1 - core) * HALF, HALF), HALF)
    return own, other


def stacked(one, two):
    def tile(j):
        ref, at = (one, two)[j // 2], (j % 2) * BLOCK
        return jnp.concatenate([ref[at : at + HALF, :], ref[at + HALF : at + BLOCK, :]], 1)

    return tile


def third_kernel(
    first, low2, top2, low3, top3, value4, value5, second, factor,
    a3, b3, c3, d3, a4, b4, c4, d4, own5, other5, own7, other7,
    kept, block4, block5, sent, value,
):
    @pl.when(lax.axis_index("row") == 2)
    def _():
        own, other = halves()
        outs = {2: kept.at[LOW, :], 3: sent.at[LOW, :], 4: block4, 5: block5}
        tiles = {
            3: (0, stacked(a3, b3), stacked(c3, d3)),
            4: (1, stacked(a4, b4), stacked(c4, d4)),
            5: (2, lambda j: own5[:, columns(j)], lambda j: other5[:, columns(j)]),
            7: (0, lambda j: own7[:, columns(j)], lambda j: other7[:, columns(j)]),
        }
        for block, ref in {2: low2, 3: low3, 4: value4, 5: value5, 6: top2, 7: top3}.items():
            value[block - 2] = ref[...]

        def apply(block, k, pair, put):
            if block in (2, 6):
                put(slice(None), product(factor[LOW if block == 2 else TOP, columns(k)], pair))
                return
            skip, mine, theirs = tiles[block]
            put(own, product(mine(k - skip), pair))
            put(other, product(theirs(k - skip), pair))

        def update(block, k, pair):
            at = block - 2

            def put(rows, change):
                value[at, rows, :] = value[at, rows, :] - change

            apply(block, k, pair, put)

        def solve(k):
            def put(rows, solved):
                outs[k][rows, :] = solved

            apply(k, k, wide(value[k - 2]), put)
            return wide(outs[k][...])

        blocks = {0: (2, 3, 6, 7), 1: (2, 3, 4, 6, 7), 2: (3, 4, 5, 6, 7), 3: (4, 5, 6, 7), 4: (5, 6, 7), 5: (6, 7)}
        for k in range(6):
            pair = wide(first[...]) if k == 0 else wide(second[...]) if k == 1 else solve(k)
            for block in blocks[k]:
                update(block, k, pair)
        kept[TOP, :] = value[4]
        sent[TOP, :] = value[5]


def line4(right_side, prev_factor, prev_solution, window_factor):
    def move(x, *pairs):
        return lax.ppermute(x, "row", list(pairs))

    def swap(x):
        return lax.ppermute(x, "col", [(0, 1), (1, 0), (2, 3), (3, 2)])

    def cross(x):
        return lax.ppermute(x, "col", [(0, 2), (2, 0), (1, 3), (3, 1)])

    half, size, six = (HALF, 4 * BLOCK), (BLOCK, WIDTH), (HALF, 6 * BLOCK)
    rows = (2 * BLOCK, WIDTH)
    pair = (2, *rows)

    def inject(up, down):
        tiles = call(tile_kernel, [rows] * 4, [pltpu.SemaphoreType.DMA((16,))], pltpu.HBM)(window_factor)
        done = [
            call(inject_kernel, [rows, rows], aliases={0: 0, 1: 1})(up[i], down[i], tiles[2 + i], tiles[i])
            for i in range(2)
        ]
        return [d[0] for d in done], [d[1] for d in done]

    def load(*earlier):
        return call(
            load_kernel,
            [prev_factor.shape, window_factor.shape, rows, half, six],
            [pltpu.SemaphoreType.DMA((5,))],
            pltpu.HBM,
        )(after(prev_factor, *earlier), window_factor, right_side)

    ups, downs, loaded = gather_row(prev_solution, 2, inject, load)
    past, factor, side, send5, send7 = loaded
    own3, own4 = downs[1], ups[2]
    own5 = move(send5, (1, 2))
    own7 = move(send7, (3, 2))
    early, late = call(early_kernel, [pair, pair])(
        past, prev_solution, *ups[1], *downs[1], ups[0][0], downs[2][0], ups[2][0], downs[0][0]
    )
    away, keep = call(late_kernel, [pair, pair])(
        past, early, late, ups[0][1], downs[2][1], ups[2][1], downs[0][1]
    )
    one, other_low, other_top = call(sum_kernel, [rows, size, size])(keep, swap(away))
    two_low, two_top = cross(other_low), cross(other_top)

    (low,) = call(first_kernel, [size])(side, one, two_low, factor)
    first = move(low, (0, 1), (3, 2))
    (top,) = call(top_kernel, [size])(side, one, two_top, factor, low)
    zero = move(low, (0, 2))
    value4 = move(top, (0, 2))
    top3 = move(top, (3, 2))
    tiles = [*own3, *own4, own5, own7]
    others = [swap(after(x, top)) for x in tiles]
    low1, top1 = call(second_kernel, [size, size])(first, low, top, factor)
    second = move(low1, (1, 2))
    value5 = move(top1, (1, 2))
    kept, block4, block5, sent = call(
        third_kernel, [rows, size, size, rows], [pltpu.VMEM((6, *size), jnp.float32)]
    )(
        zero, low, top, first, top3, value4, value5, second, factor,
        *tiles[:2], *others[:2], *tiles[2:4], *others[2:4], own5, others[4], own7, others[5],
    )
    last = move(sent, (2, 3))
    block5 = move(block5, (2, 1))
    block4 = move(block4, (2, 0))
    return call(last_kernel, [rows], inside=False)(low, low1, kept, last, block4, block5)[0]


def body(right_side, prev_factor, prev_solution, window_factor):
    blocks = window_factor.shape[1] // STEPS
    slots = right_side.shape[0] // blocks
    if lax.axis_size("row") == 4 and lax.axis_size("col") == 4 and slots == 2:
        return line4(right_side, prev_factor, prev_solution, window_factor)
    return general(right_side, prev_factor, prev_solution, window_factor)


def solution(mesh):
    in_specs = (
        P(("groups", "row"), None),
        P(("groups", "row"), "col"),
        P(("groups", "col"), "row"),
        P(("groups", "row"), None),
    )
    out_specs = P(("groups", "row"), "col")
    return jax.shard_map(body, mesh=mesh, in_specs=in_specs, out_specs=out_specs, check_vma=False)
```

```python
import jax
import jax.numpy as jnp
from jax import lax
from jax.experimental import pallas as pl
from jax.experimental.pallas import tpu as pltpu
from jax.sharding import PartitionSpec as P

NRHS = 512
STEPS = 6
HIGH = lax.Precision.HIGH


def mul(a, b):
    return jnp.dot(a, b, precision=HIGH, preferred_element_type=jnp.float32)


def general(right_side, prev_factor, prev_solution, window_factor):
    row_count = lax.axis_size("row")
    row_index = lax.axis_index("row")
    col_count = lax.axis_size("col")
    col_index = lax.axis_index("col")
    blocks = window_factor.shape[1] // STEPS
    slots = right_side.shape[0] // blocks
    width = NRHS // col_count
    partial_value = mul(prev_factor, lax.all_gather(prev_solution, "row", axis=1, tiled=True))
    prior = lax.psum_scatter(partial_value, "col", scatter_dimension=1, tiled=True)
    mine = lax.dynamic_slice_in_dim(right_side, col_index * width, width, 1)
    resid = (mine - prior).reshape(slots, blocks, width)
    tiles = window_factor.reshape(slots, blocks, STEPS, blocks)
    order = jnp.arange(slots, dtype=jnp.int32) * row_count + row_index
    for step in range(STEPS):
        root = step % row_count
        solved = mul(tiles[step // row_count, :, step, :], resid[step // row_count])
        solved = lax.psum(jnp.where(row_index == root, solved, jnp.zeros_like(solved)), "row")
        update = jnp.einsum("sij,jn->sin", tiles[:, :, step, :], solved, precision=HIGH)
        resid = jnp.where((order > step)[:, None, None], resid - update, resid)
        resid = jnp.where((order == step)[:, None, None], solved[None], resid)
    return resid.reshape(slots * blocks, width)


BLOCK = 256
HALF = BLOCK // 2
WIDTH = 128
VMEM_SPEC = pl.BlockSpec(memory_space=pltpu.VMEM)


def after(x, *earlier):
    return lax.optimization_barrier((x, *earlier))[0]


def split(x):
    high = x.astype(jnp.bfloat16)
    return high, (x - high.astype(jnp.float32)).astype(jnp.bfloat16)


def wide(x):
    return jnp.concatenate(split(x), 1)


def product(tile, pair):
    high, low = split(tile)
    both = jnp.dot(high, pair, preferred_element_type=jnp.float32)
    both = both + jnp.dot(low, pair, preferred_element_type=jnp.float32)
    return both[:, :WIDTH] + both[:, WIDTH:]


def columns(k):
    return slice(k * BLOCK, (k + 1) * BLOCK)


LOW, TOP = slice(0, BLOCK), slice(BLOCK, 2 * BLOCK)


def call(kernel, shapes, scratch=(), space=pltpu.VMEM, inside=True, aliases={}):
    def run(*args):
        return pl.pallas_call(
            kernel,
            out_shape=[(pltpu.VMEM if inside else jax.ShapeDtypeStruct)(s, jnp.float32) for s in shapes],
            in_specs=[pl.BlockSpec(memory_space=space)] * len(args),
            out_specs=[VMEM_SPEC] * len(shapes),
            scratch_shapes=list(scratch),
            input_output_aliases=aliases,
            compiler_params=pltpu.CompilerParams(vmem_limit_bytes=32 * 1024 * 1024),
        )(*[pltpu.with_memory_space_constraint(a, space) for a in args])

    return run


def sent_rows():
    core = lax.axis_index("col") % 2
    low = pl.ds(pl.multiple_of(core * HALF, HALF), HALF)
    return low, pl.ds(pl.multiple_of(BLOCK + core * HALF, HALF), HALF)


def copy_all(pairs, sem):
    copies = [pltpu.make_async_copy(s, d, sem.at[i]) for i, (s, d) in enumerate(pairs)]
    for copy in copies:
        copy.start()
    for copy in copies:
        copy.wait()


def stack_copies(source, rows, start, out, count=8):
    return [
        (source.at[rows, pl.ds(start + j * HALF, HALF)], out.at[slice(j * HALF, (j + 1) * HALF), :])
        for j in range(count)
    ]


def tile_kernel(factor, three, four, sem):
    low, top = sent_rows()
    copy_all(stack_copies(factor, low, 0, three) + stack_copies(factor, top, BLOCK, four), sem)


def inject_kernel(x_in, three, four, x):
    @pl.when(lax.axis_index("row") == 0)
    def _():
        x[...] = four[...]

    @pl.when(lax.axis_index("row") == 3)
    def _():
        x[...] = three[...]


def inject_seven_kernel(x_in, seven, x):
    @pl.when(lax.axis_index("row") == 3)
    def _():
        x[...] = seven[...]


def load_kernel(past, factor, side, past_out, factor_out, side_out, five, seven, eight, sem):
    _, top = sent_rows()
    mine = pl.ds(pl.multiple_of(lax.axis_index("col") * WIDTH, WIDTH), WIDTH)
    copy_all(
        stack_copies(factor, top, 0, seven)
        + [
            (past, past_out),
            (factor, factor_out),
            (side.at[:, mine], side_out),
        ]
        + stack_copies(factor, top, 2 * BLOCK, five)
        + stack_copies(factor, top, 4 * BLOCK, eight, 4),
        sem,
    )


def spread(factor, *parts):
    high, low = split(factor)
    pair = jnp.concatenate([wide(x) for x in parts], 1)
    both = jnp.dot(high, pair, preferred_element_type=jnp.float32)
    both = both + jnp.dot(low, pair, preferred_element_type=jnp.float32)
    lanes = [both[:, i * WIDTH : (i + 1) * WIDTH] for i in range(2 * len(parts))]
    return [lanes[2 * i] + lanes[2 * i + 1] for i in range(len(parts))]


def at_end():
    row_index = lax.axis_index("row")
    return jnp.logical_or(row_index == 0, row_index == 3)


def early_kernel(past, own, edge1, edge2, middle2, early):
    got = spread(past[...], own[...], jnp.where(at_end(), edge2[...], middle2[...]), edge1[...])
    for i in range(3):
        early[i] = got[i]


def late_kernel(past, early, edge3, middle3, away, keep):
    row_index, col_index = lax.axis_index("row"), lax.axis_index("col")
    keeps_even = lax.rem(col_index, 2) == lax.rem(row_index, 2)
    (three,) = spread(past[...], jnp.where(at_end(), edge3[...], middle3[...]))
    near = lax.div(row_index, 2) == lax.div(col_index, 2)
    even = [jnp.where(near, early[0], early[1]), jnp.where(near, early[1], early[0])]
    odd = [jnp.where(near, early[2], three), jnp.where(near, three, early[2])]
    for i in range(2):
        away[i] = jnp.where(keeps_even, odd[i], even[i])
        keep[i] = jnp.where(keeps_even, even[i], odd[i])


def sum_kernel(keep, came, own, other_low, other_top):
    own[...] = keep[0] + came[0]
    other_low[...] = keep[1, LOW] + came[1, LOW]
    other_top[...] = keep[1, TOP] + came[1, TOP]


def first_kernel(side, one, two, factor, low):
    low[...] = side[LOW, :] - (one[LOW, :] + two[...])

    @pl.when(lax.axis_index("row") == 0)
    def _():
        low[...] = product(factor[LOW, columns(0)], wide(low[...]))


def top_kernel(side, one, two, factor, low, top):
    top[...] = side[TOP, :] - (one[TOP, :] + two[...])

    @pl.when(lax.axis_index("row") == 0)
    def _():
        top[...] = top[...] - product(factor[TOP, columns(0)], wide(low[...]))


def second_kernel(solved, low_in, factor, low):
    @pl.when(lax.axis_index("row") == 1)
    def _():
        value = low_in[...] - product(factor[LOW, columns(0)], wide(solved[...]))
        low[LOW, :] = solved[...]
        low[TOP, :] = product(factor[LOW, columns(1)], wide(value))


def five_kernel(solved, top_in, factor, top):
    @pl.when(lax.axis_index("row") == 1)
    def _():
        value = top_in[...] - product(factor[TOP, columns(0)], wide(solved[LOW, :]))
        top[...] = value - product(factor[TOP, columns(1)], wide(solved[TOP, :]))


def last_kernel(low, low1, low2, top2, last, block4, block5, out):
    row_index = lax.axis_index("row")

    @pl.when(row_index == 0)
    def _():
        out[LOW, :] = low[...]
        out[TOP, :] = block4[...]

    @pl.when(row_index == 1)
    def _():
        out[LOW, :] = low1[TOP, :]
        out[TOP, :] = block5[...]

    @pl.when(row_index == 2)
    def _():
        out[LOW, :] = low2[...]
        out[TOP, :] = top2[...]

    @pl.when(row_index == 3)
    def _():
        out[...] = last[...]


def halves():
    core = lax.axis_index("col") % 2
    own = pl.ds(pl.multiple_of(core * HALF, HALF), HALF)
    other = pl.ds(pl.multiple_of((1 - core) * HALF, HALF), HALF)
    return own, other


def stacked(ref, j):
    return jnp.concatenate([ref[j * BLOCK : j * BLOCK + HALF, :], ref[j * BLOCK + HALF : (j + 1) * BLOCK, :]], 1)


def join_kernel(*refs):
    out, at = refs[-1], 0
    for ref in refs[:-1]:
        out[at : at + ref.shape[0], :] = ref[...]
        at += ref.shape[0]


def third_kernel(first, second, low2, factor, mine3, theirs3, block2, block3, value):
    @pl.when(lax.axis_index("row") == 2)
    def _():
        own, other = halves()
        pairs = [wide(second[LOW, :]), wide(second[TOP, :])]
        start = low2[...]
        for k in range(2):
            start = start - product(factor[LOW, columns(k)], pairs[k])
        block2[...] = product(factor[LOW, columns(2)], wide(start))
        pairs.append(wide(block2[...]))
        for rows, ref in ((own, mine3), (other, theirs3)):
            start = first[rows, :]
            for k in range(3):
                start = start - product(stacked(ref, k), pairs[k])
            value[rows, :] = start
        pair = wide(value[...])
        block3[own, :] = product(stacked(mine3, 3), pair)
        block3[other, :] = product(stacked(theirs3, 3), pair)


def fourth_kernel(
    second, block2, block3, top2, value4, value5, top3, factor,
    mine37, theirs37, mine458, theirs458,
    kept, block4, block5, sent, value,
):
    @pl.when(lax.axis_index("row") == 2)
    def _():
        own, other = halves()
        sides = ((own, mine37, mine458), (other, theirs37, theirs458))
        pairs = [wide(x) for x in (second[LOW, :], second[TOP, :], block2[...], block3[...])]
        for rows, _, tiles in sides:
            start = value4[rows, :]
            for k in range(1, 4):
                start = start - product(stacked(tiles, k - 1), pairs[k])
            value[rows, :] = start
        pair = wide(value[...])
        for rows, _, tiles in sides:
            block4[rows, :] = product(stacked(tiles, 3), pair)
        pairs.append(wide(block4[...]))
        for rows, _, tiles in sides:
            start = value5[rows, :]
            for k in range(2, 5):
                start = start - product(stacked(tiles, 4 + k - 2), pairs[k])
            value[rows, :] = start
        pair = wide(value[...])
        for rows, _, tiles in sides:
            block5[rows, :] = product(stacked(tiles, 7), pair)
        pairs.append(wide(block5[...]))
        start = top2[...]
        for k in range(6):
            start = start - product(factor[TOP, columns(k)], pairs[k])
        kept[...] = start
        sent[LOW, :] = block3[...]
        for rows, sevens, tiles in sides:
            start = top3[rows, :]
            for k in range(6):
                tile = stacked(sevens, 4 + k) if k < 4 else stacked(tiles, 8 + k - 4)
                start = start - product(tile, pairs[k])
            value[rows, :] = start
        sent[TOP, :] = value[...]


def line4(right_side, prev_factor, prev_solution, window_factor):
    def move(x, *pairs):
        return lax.ppermute(x, "row", list(pairs))

    def swap(x):
        return lax.ppermute(x, "col", [(0, 1), (1, 0), (2, 3), (3, 2)])

    def cross(x):
        return lax.ppermute(x, "col", [(0, 2), (2, 0), (1, 3), (3, 1)])

    def edges(x):
        return move(x, (0, 1), (1, 0), (2, 3), (3, 2))

    def middle(x):
        return move(x, (1, 2), (2, 1))

    size, rows, tall = (BLOCK, WIDTH), (2 * BLOCK, WIDTH), prev_solution.shape
    dma = pltpu.SemaphoreType.DMA

    edge1 = edges(prev_solution)
    send3, send4 = call(tile_kernel, [tall, tall], [dma((16,))], pltpu.HBM)(window_factor)
    middle3 = middle(after(prev_solution, send3))
    (carried,) = call(inject_kernel, [tall], aliases={0: 0})(middle3, send3, send4)
    edge2 = edges(carried)
    middle2 = middle(edge1)
    past, factor, side, send5, send7, send8 = call(
        load_kernel,
        [prev_factor.shape, window_factor.shape, rows, tall, tall, rows],
        [dma((23,))],
        pltpu.HBM,
    )(after(prev_factor, carried, edge1), window_factor, right_side)
    (carried,) = call(inject_seven_kernel, [tall], aliases={0: 0})(middle2, send7)
    middle2 = carried
    edge3 = edges(carried)
    (mine37,) = call(join_kernel, [(2 * tall[0], WIDTH)])(edge2, edge3)
    own4 = move(edge2, (1, 2))
    own5 = move(send5, (1, 2))
    own8 = move(send8, (3, 2))

    (early,) = call(early_kernel, [(3, *rows)])(past, prev_solution, edge1, edge2, middle2)
    away, keep = call(late_kernel, [(2, *rows)] * 2)(past, early, edge3, middle3)
    one, other_low, other_top = call(sum_kernel, [rows, size, size])(after(keep, own5), swap(away))
    two_low, two_top = cross(other_low), cross(other_top)
    (low,) = call(first_kernel, [size])(side, one, two_low, factor)
    first = move(low, (0, 1), (3, 2))
    (top,) = call(top_kernel, [size])(side, one, two_top, factor, low)
    value4 = move(top, (0, 2))
    top3 = move(top, (3, 2))
    (low1,) = call(second_kernel, [rows])(first, after(low, own4, own8), factor)
    second = move(low1, (1, 2))
    (top1,) = call(five_kernel, [size])(low1, top, factor)
    value5 = move(top1, (1, 2))
    theirs37 = swap(after(mine37, one))
    (mine458,) = call(join_kernel, [(2 * tall[0] + rows[0], WIDTH)])(own4, own5, own8)
    theirs458 = swap(after(mine458, low1))
    block2, block3 = call(third_kernel, [size, size], [pltpu.VMEM(size, jnp.float32)])(
        first, second, low, factor, mine37, theirs37
    )
    kept, block4, block5, sent = call(
        fourth_kernel, [size, size, size, rows], [pltpu.VMEM(size, jnp.float32)]
    )(
        second, block2, block3, top, value4, value5, top3, factor,
        mine37, theirs37, mine458, theirs458,
    )
    last = move(sent, (2, 3))
    block5 = move(block5, (2, 1))
    block4 = move(block4, (2, 0))
    return call(last_kernel, [rows], inside=False)(low, low1, block2, kept, last, block4, block5)[0]


def body(right_side, prev_factor, prev_solution, window_factor):
    blocks = window_factor.shape[1] // STEPS
    slots = right_side.shape[0] // blocks
    if lax.axis_size("row") == 4 and lax.axis_size("col") == 4 and slots == 2:
        return line4(right_side, prev_factor, prev_solution, window_factor)
    return general(right_side, prev_factor, prev_solution, window_factor)


def solution(mesh):
    in_specs = (
        P(("groups", "row"), None),
        P(("groups", "row"), "col"),
        P(("groups", "col"), "row"),
        P(("groups", "row"), None),
    )
    out_specs = P(("groups", "row"), "col")
    return jax.shard_map(body, mesh=mesh, in_specs=in_specs, out_specs=out_specs, check_vma=False)
```

```python
import jax
import jax.numpy as jnp
from jax import lax
from jax.experimental import pallas as pl
from jax.experimental.pallas import tpu as pltpu
from jax.sharding import PartitionSpec as P

NRHS = 512
STEPS = 6
HIGH = lax.Precision.HIGH


def mul(a, b):
    return jnp.dot(a, b, precision=HIGH, preferred_element_type=jnp.float32)


def general(right_side, prev_factor, prev_solution, window_factor):
    row_count = lax.axis_size("row")
    row_index = lax.axis_index("row")
    col_count = lax.axis_size("col")
    col_index = lax.axis_index("col")
    blocks = window_factor.shape[1] // STEPS
    slots = right_side.shape[0] // blocks
    width = NRHS // col_count
    partial_value = mul(prev_factor, lax.all_gather(prev_solution, "row", axis=1, tiled=True))
    prior = lax.psum_scatter(partial_value, "col", scatter_dimension=1, tiled=True)
    mine = lax.dynamic_slice_in_dim(right_side, col_index * width, width, 1)
    resid = (mine - prior).reshape(slots, blocks, width)
    tiles = window_factor.reshape(slots, blocks, STEPS, blocks)
    order = jnp.arange(slots, dtype=jnp.int32) * row_count + row_index
    for step in range(STEPS):
        root = step % row_count
        solved = mul(tiles[step // row_count, :, step, :], resid[step // row_count])
        solved = lax.psum(jnp.where(row_index == root, solved, jnp.zeros_like(solved)), "row")
        update = jnp.einsum("sij,jn->sin", tiles[:, :, step, :], solved, precision=HIGH)
        resid = jnp.where((order > step)[:, None, None], resid - update, resid)
        resid = jnp.where((order == step)[:, None, None], solved[None], resid)
    return resid.reshape(slots * blocks, width)


BLOCK = 256
HALF = BLOCK // 2
WIDTH = 128
VMEM_SPEC = pl.BlockSpec(memory_space=pltpu.VMEM)


def after(x, *earlier):
    return lax.optimization_barrier((x, *earlier))[0]


def split(x):
    high = x.astype(jnp.bfloat16)
    return high, (x - high.astype(jnp.float32)).astype(jnp.bfloat16)


def wide(x):
    return jnp.concatenate(split(x), 1)


def product(tile, pair):
    high, low = split(tile)
    both = jnp.dot(high, pair, preferred_element_type=jnp.float32)
    both = both + jnp.dot(low, pair, preferred_element_type=jnp.float32)
    return both[:, :WIDTH] + both[:, WIDTH:]


def columns(k):
    return slice(k * BLOCK, (k + 1) * BLOCK)


LOW, TOP = slice(0, BLOCK), slice(BLOCK, 2 * BLOCK)


def call(kernel, shapes, scratch=(), space=pltpu.VMEM, inside=True, aliases={}):
    def run(*args):
        spaces = space if isinstance(space, list) else [space] * len(args)
        return pl.pallas_call(
            kernel,
            out_shape=[(pltpu.VMEM if inside else jax.ShapeDtypeStruct)(s, jnp.float32) for s in shapes],
            in_specs=[pl.BlockSpec(memory_space=m) for m in spaces],
            out_specs=[VMEM_SPEC] * len(shapes),
            scratch_shapes=list(scratch),
            input_output_aliases=aliases,
            compiler_params=pltpu.CompilerParams(vmem_limit_bytes=32 * 1024 * 1024),
        )(*[pltpu.with_memory_space_constraint(a, m) for a, m in zip(args, spaces)])

    return run


def sent_rows():
    core = lax.axis_index("col") % 2
    low = pl.ds(pl.multiple_of(core * HALF, HALF), HALF)
    return low, pl.ds(pl.multiple_of(BLOCK + core * HALF, HALF), HALF)


def copy_all(pairs, sem):
    copies = [pltpu.make_async_copy(s, d, sem.at[i]) for i, (s, d) in enumerate(pairs)]
    for copy in copies:
        copy.start()
    for copy in copies:
        copy.wait()


def stack_copies(source, rows, start, out, count=8):
    return [
        (source.at[rows, pl.ds(start + j * HALF, HALF)], out.at[slice(j * HALF, (j + 1) * HALF), :])
        for j in range(count)
    ]


def inject_kernel(x_in, factor, x, sem):
    low, top = sent_rows()

    @pl.when(lax.axis_index("row") == 0)
    def _():
        copy_all(stack_copies(factor, top, BLOCK, x), sem)

    @pl.when(lax.axis_index("row") == 3)
    def _():
        copy_all(stack_copies(factor, low, 0, x), sem)


def inject_seven_kernel(x_in, seven, x):
    @pl.when(lax.axis_index("row") == 3)
    def _():
        x[...] = seven[...]


def load_kernel(past, factor, side, past_out, factor_out, side_out, five, seven, eight, sem):
    _, top = sent_rows()
    mine = pl.ds(pl.multiple_of(lax.axis_index("col") * WIDTH, WIDTH), WIDTH)
    copy_all(
        stack_copies(factor, top, 0, seven)
        + [
            (past, past_out),
            (factor, factor_out),
            (side.at[:, mine], side_out),
        ]
        + stack_copies(factor, top, 2 * BLOCK, five)
        + stack_copies(factor, top, 4 * BLOCK, eight, 4),
        sem,
    )


def spread(factor, *parts):
    high, low = split(factor)
    pair = jnp.concatenate([wide(x) for x in parts], 1)
    both = jnp.dot(high, pair, preferred_element_type=jnp.float32)
    both = both + jnp.dot(low, pair, preferred_element_type=jnp.float32)
    lanes = [both[:, i * WIDTH : (i + 1) * WIDTH] for i in range(2 * len(parts))]
    return [lanes[2 * i] + lanes[2 * i + 1] for i in range(len(parts))]


def at_end():
    row_index = lax.axis_index("row")
    return jnp.logical_or(row_index == 0, row_index == 3)


def early_kernel(past, own, edge1, edge2, middle2, early):
    got = spread(past[...], own[...], jnp.where(at_end(), edge2[...], middle2[...]), edge1[...])
    for i in range(3):
        early[i] = got[i]


def late_kernel(past, early, edge3, middle3, away, keep):
    row_index, col_index = lax.axis_index("row"), lax.axis_index("col")
    keeps_even = lax.rem(col_index, 2) == lax.rem(row_index, 2)
    (three,) = spread(past[...], jnp.where(at_end(), edge3[...], middle3[...]))
    near = lax.div(row_index, 2) == lax.div(col_index, 2)
    even = [jnp.where(near, early[0], early[1]), jnp.where(near, early[1], early[0])]
    odd = [jnp.where(near, early[2], three), jnp.where(near, three, early[2])]
    for i in range(2):
        away[i] = jnp.where(keeps_even, odd[i], even[i])
        keep[i] = jnp.where(keeps_even, even[i], odd[i])


def sum_kernel(keep, came, own, other_low, other_top):
    own[...] = keep[0] + came[0]
    other_low[...] = keep[1, LOW] + came[1, LOW]
    other_top[...] = keep[1, TOP] + came[1, TOP]


def first_kernel(side, one, two, factor, low):
    low[...] = side[LOW, :] - (one[LOW, :] + two[...])

    @pl.when(lax.axis_index("row") == 0)
    def _():
        low[...] = product(factor[LOW, columns(0)], wide(low[...]))


def top_kernel(side, one, two, factor, low, top):
    top[...] = side[TOP, :] - (one[TOP, :] + two[...])

    @pl.when(lax.axis_index("row") == 0)
    def _():
        top[...] = top[...] - product(factor[TOP, columns(0)], wide(low[...]))


def second_kernel(solved, low_in, factor, low):
    @pl.when(lax.axis_index("row") == 1)
    def _():
        value = low_in[...] - product(factor[LOW, columns(0)], wide(solved[...]))
        low[LOW, :] = solved[...]
        low[TOP, :] = product(factor[LOW, columns(1)], wide(value))


def five_kernel(solved, top_in, factor, top):
    @pl.when(lax.axis_index("row") == 1)
    def _():
        value = top_in[...] - product(factor[TOP, columns(0)], wide(solved[LOW, :]))
        top[...] = value - product(factor[TOP, columns(1)], wide(solved[TOP, :]))


def last_kernel(low, low1, low2, top2, last3, last7, block4, block5, out):
    row_index = lax.axis_index("row")

    @pl.when(row_index == 0)
    def _():
        out[LOW, :] = low[...]
        out[TOP, :] = block4[...]

    @pl.when(row_index == 1)
    def _():
        out[LOW, :] = low1[TOP, :]
        out[TOP, :] = block5[...]

    @pl.when(row_index == 2)
    def _():
        out[LOW, :] = low2[...]
        out[TOP, :] = top2[...]

    @pl.when(row_index == 3)
    def _():
        out[LOW, :] = last3[...]
        out[TOP, :] = last7[...]


def halves():
    core = lax.axis_index("col") % 2
    own = pl.ds(pl.multiple_of(core * HALF, HALF), HALF)
    other = pl.ds(pl.multiple_of((1 - core) * HALF, HALF), HALF)
    return own, other


def stacked(ref, j):
    return jnp.concatenate([ref[j * BLOCK : j * BLOCK + HALF, :], ref[j * BLOCK + HALF : (j + 1) * BLOCK, :]], 1)


def join_kernel(*refs):
    out, at = refs[-1], 0
    for ref in refs[:-1]:
        out[at : at + ref.shape[0], :] = ref[...]
        at += ref.shape[0]


def third_kernel(first, second, low2, factor, mine, theirs, block2, block3, value):
    @pl.when(lax.axis_index("row") == 2)
    def _():
        own, other = halves()
        pairs = [wide(second[LOW, :]), wide(second[TOP, :])]
        start = low2[...]
        for k in range(2):
            start = start - product(factor[LOW, columns(k)], pairs[k])
        block2[...] = product(factor[LOW, columns(2)], wide(start))
        pairs.append(wide(block2[...]))
        for rows, ref in ((own, mine), (other, theirs)):
            start = first[rows, :]
            for k in range(3):
                start = start - product(stacked(ref, k), pairs[k])
            value[rows, :] = start
        pair = wide(value[...])
        block3[own, :] = product(stacked(mine, 3), pair)
        block3[other, :] = product(stacked(theirs, 3), pair)


def fourth_kernel(
    second, block2, block3, top2, value4, value5, top3, factor,
    mine, theirs,
    kept, block4, block5, sent, value,
):
    @pl.when(lax.axis_index("row") == 2)
    def _():
        own, other = halves()
        sides = ((own, mine), (other, theirs))
        pairs = [wide(x) for x in (second[LOW, :], second[TOP, :], block2[...], block3[...])]
        for rows, tiles in sides:
            start = value4[rows, :]
            for k in range(1, 4):
                start = start - product(stacked(tiles, 10 + k - 1), pairs[k])
            value[rows, :] = start
        pair = wide(value[...])
        for rows, tiles in sides:
            block4[rows, :] = product(stacked(tiles, 13), pair)
        pairs.append(wide(block4[...]))
        for rows, tiles in sides:
            start = value5[rows, :]
            for k in range(2, 5):
                start = start - product(stacked(tiles, 14 + k - 2), pairs[k])
            value[rows, :] = start
        pair = wide(value[...])
        for rows, tiles in sides:
            block5[rows, :] = product(stacked(tiles, 17), pair)
        pairs.append(wide(block5[...]))
        start = top2[...]
        for k in range(6):
            start = start - product(factor[TOP, columns(k)], pairs[k])
        kept[...] = start
        for rows, tiles in sides:
            start = top3[rows, :]
            for k in range(6):
                start = start - product(stacked(tiles, 4 + k), pairs[k])
            sent[rows, :] = start


def line4(right_side, prev_factor, prev_solution, window_factor):
    def move(x, *pairs):
        return lax.ppermute(x, "row", list(pairs))

    def swap(x):
        return lax.ppermute(x, "col", [(0, 1), (1, 0), (2, 3), (3, 2)])

    def cross(x):
        return lax.ppermute(x, "col", [(0, 2), (2, 0), (1, 3), (3, 1)])

    def edges(x):
        return move(x, (0, 1), (1, 0), (2, 3), (3, 2))

    def middle(x):
        return move(x, (1, 2), (2, 1))

    size, rows, tall = (BLOCK, WIDTH), (2 * BLOCK, WIDTH), prev_solution.shape
    dma = pltpu.SemaphoreType.DMA

    edge1 = edges(prev_solution)
    middle3 = middle(prev_solution)
    (carried,) = call(inject_kernel, [tall], [dma((8,))], [pltpu.VMEM, pltpu.HBM], aliases={0: 0})(
        middle3, window_factor
    )
    edge2 = edges(carried)
    middle2 = middle(edge1)
    past, factor, side, send5, send7, send8 = call(
        load_kernel,
        [prev_factor.shape, window_factor.shape, rows, tall, tall, rows],
        [dma((23,))],
        pltpu.HBM,
    )(after(prev_factor, carried, edge1), window_factor, right_side)
    (carried,) = call(inject_seven_kernel, [tall], aliases={0: 0})(middle2, send7)
    middle2 = carried
    edge3 = edges(carried)

    (early,) = call(early_kernel, [(3, *rows)])(past, prev_solution, edge1, edge2, middle2)
    (send45,) = call(join_kernel, [(2 * tall[0], WIDTH)])(after(edge2, early), send5)
    mine45 = move(send45, (1, 2))
    away, keep = call(late_kernel, [(2, *rows)] * 2)(past, early, edge3, middle3)
    one, other_low, other_top = call(sum_kernel, [rows, size, size])(keep, swap(away))
    two_low, two_top = cross(other_low), cross(other_top)
    own8 = move(after(send8, one), (3, 2))
    (low,) = call(first_kernel, [size])(side, one, two_low, factor)
    first = move(low, (0, 1), (3, 2))
    (top,) = call(top_kernel, [size])(side, one, two_top, factor, low)
    value4 = move(top, (0, 2))
    top3 = move(top, (3, 2))
    (mine,) = call(join_kernel, [(4 * tall[0] + rows[0], WIDTH)])(edge2, edge3, own8, after(mine45, first, top))
    theirs = swap(mine)
    (low1,) = call(second_kernel, [rows])(first, after(low, top), factor)
    second = move(low1, (1, 2))
    (top1,) = call(five_kernel, [size])(low1, top, factor)
    value5 = move(top1, (1, 2))
    block2, block3 = call(third_kernel, [size, size], [pltpu.VMEM(size, jnp.float32)])(
        first, second, low, factor, mine, theirs
    )
    last3 = move(block3, (2, 3))
    kept, block4, block5, sent = call(
        fourth_kernel, [size] * 4, [pltpu.VMEM(size, jnp.float32)]
    )(
        second, block2, block3, top, value4, value5, top3, factor, mine, theirs
    )
    last7 = move(sent, (2, 3))
    block5 = move(block5, (2, 1))
    block4 = move(block4, (2, 0))
    return call(last_kernel, [rows], inside=False)(
        low, low1, block2, kept, last3, last7, block4, block5
    )[0]


def body(right_side, prev_factor, prev_solution, window_factor):
    blocks = window_factor.shape[1] // STEPS
    slots = right_side.shape[0] // blocks
    if lax.axis_size("row") == 4 and lax.axis_size("col") == 4 and slots == 2:
        return line4(right_side, prev_factor, prev_solution, window_factor)
    return general(right_side, prev_factor, prev_solution, window_factor)


def solution(mesh):
    in_specs = (
        P(("groups", "row"), None),
        P(("groups", "row"), "col"),
        P(("groups", "col"), "row"),
        P(("groups", "row"), None),
    )
    out_specs = P(("groups", "row"), "col")
    return jax.shard_map(body, mesh=mesh, in_specs=in_specs, out_specs=out_specs, check_vma=False)
```

```python
import jax
import jax.numpy as jnp
from jax import lax
from jax.experimental import pallas as pl
from jax.experimental.pallas import tpu as pltpu
from jax.sharding import PartitionSpec as P

NRHS = 512
STEPS = 6
HIGH = lax.Precision.HIGH


def mul(a, b):
    return jnp.dot(a, b, precision=HIGH, preferred_element_type=jnp.float32)


def general(right_side, prev_factor, prev_solution, window_factor):
    row_count = lax.axis_size("row")
    row_index = lax.axis_index("row")
    col_count = lax.axis_size("col")
    col_index = lax.axis_index("col")
    blocks = window_factor.shape[1] // STEPS
    slots = right_side.shape[0] // blocks
    width = NRHS // col_count
    partial_value = mul(prev_factor, lax.all_gather(prev_solution, "row", axis=1, tiled=True))
    prior = lax.psum_scatter(partial_value, "col", scatter_dimension=1, tiled=True)
    mine = lax.dynamic_slice_in_dim(right_side, col_index * width, width, 1)
    resid = (mine - prior).reshape(slots, blocks, width)
    tiles = window_factor.reshape(slots, blocks, STEPS, blocks)
    order = jnp.arange(slots, dtype=jnp.int32) * row_count + row_index
    for step in range(STEPS):
        root = step % row_count
        solved = mul(tiles[step // row_count, :, step, :], resid[step // row_count])
        solved = lax.psum(jnp.where(row_index == root, solved, jnp.zeros_like(solved)), "row")
        update = jnp.einsum("sij,jn->sin", tiles[:, :, step, :], solved, precision=HIGH)
        resid = jnp.where((order > step)[:, None, None], resid - update, resid)
        resid = jnp.where((order == step)[:, None, None], solved[None], resid)
    return resid.reshape(slots * blocks, width)


BLOCK = 256
HALF = BLOCK // 2
WIDTH = 128
VMEM_SPEC = pl.BlockSpec(memory_space=pltpu.VMEM)


def after(x, *earlier):
    return lax.optimization_barrier((x, *earlier))[0]


def split(x):
    high = x.astype(jnp.bfloat16)
    return high, (x - high.astype(jnp.float32)).astype(jnp.bfloat16)


def wide(x):
    return jnp.concatenate(split(x), 1)


def product(tile, pair):
    high, low = split(tile)
    both = jnp.dot(high, pair, preferred_element_type=jnp.float32)
    both = both + jnp.dot(low, pair, preferred_element_type=jnp.float32)
    return both[:, :WIDTH] + both[:, WIDTH:]


def columns(k):
    return slice(k * BLOCK, (k + 1) * BLOCK)


LOW, TOP = slice(0, BLOCK), slice(BLOCK, 2 * BLOCK)


def call(kernel, shapes, scratch=(), space=pltpu.VMEM, inside=True, aliases={}):
    def run(*args):
        spaces = space if isinstance(space, list) else [space] * len(args)
        return pl.pallas_call(
            kernel,
            out_shape=[(pltpu.VMEM if inside else jax.ShapeDtypeStruct)(s, jnp.float32) for s in shapes],
            in_specs=[pl.BlockSpec(memory_space=m) for m in spaces],
            out_specs=[VMEM_SPEC] * len(shapes),
            scratch_shapes=list(scratch),
            input_output_aliases=aliases,
            compiler_params=pltpu.CompilerParams(vmem_limit_bytes=32 * 1024 * 1024),
        )(*[pltpu.with_memory_space_constraint(a, m) for a, m in zip(args, spaces)])

    return run


def sent_rows():
    core = lax.axis_index("col") % 2
    low = pl.ds(pl.multiple_of(core * HALF, HALF), HALF)
    return low, pl.ds(pl.multiple_of(BLOCK + core * HALF, HALF), HALF)


def copy_all(pairs, sem):
    copies = [pltpu.make_async_copy(s, d, sem.at[i]) for i, (s, d) in enumerate(pairs)]
    for copy in copies:
        copy.start()
    for copy in copies:
        copy.wait()


def stack_copies(source, rows, start, out, count=8):
    return [
        (source.at[rows, pl.ds(start + j * HALF, HALF)], out.at[slice(j * HALF, (j + 1) * HALF), :])
        for j in range(count)
    ]


def inject_kernel(x_in, factor, x, sem):
    low, top = sent_rows()

    @pl.when(lax.axis_index("row") == 0)
    def _():
        copy_all(stack_copies(factor, top, BLOCK, x), sem)

    @pl.when(lax.axis_index("row") == 3)
    def _():
        copy_all(stack_copies(factor, low, 0, x), sem)


def inject_seven_kernel(x_in, seven, x):
    @pl.when(lax.axis_index("row") == 3)
    def _():
        x[...] = seven[...]


def load_kernel(past, factor, side, past_out, factor_out, side_out, five, seven, eight, sem):
    _, top = sent_rows()
    mine = pl.ds(pl.multiple_of(lax.axis_index("col") * WIDTH, WIDTH), WIDTH)
    copy_all(
        stack_copies(factor, top, 0, seven)
        + [
            (past, past_out),
            (factor, factor_out),
            (side.at[:, mine], side_out),
        ]
        + stack_copies(factor, top, 2 * BLOCK, five)
        + stack_copies(factor, top, 4 * BLOCK, eight, 4),
        sem,
    )


def spread(factor, *parts):
    high, low = split(factor)
    pair = jnp.concatenate([wide(x) for x in parts], 1)
    both = jnp.dot(high, pair, preferred_element_type=jnp.float32)
    both = both + jnp.dot(low, pair, preferred_element_type=jnp.float32)
    lanes = [both[:, i * WIDTH : (i + 1) * WIDTH] for i in range(2 * len(parts))]
    return [lanes[2 * i] + lanes[2 * i + 1] for i in range(len(parts))]


def at_end():
    row_index = lax.axis_index("row")
    return jnp.logical_or(row_index == 0, row_index == 3)


def early_kernel(past, own, edge1, edge2, middle2, early):
    got = spread(past[...], own[...], jnp.where(at_end(), edge2[...], middle2[...]), edge1[...])
    for i in range(3):
        early[i] = got[i]


def late_kernel(past, early, edge3, middle3, away, keep):
    row_index, col_index = lax.axis_index("row"), lax.axis_index("col")
    keeps_even = lax.rem(col_index, 2) == lax.rem(row_index, 2)
    (three,) = spread(past[...], jnp.where(at_end(), edge3[...], middle3[...]))
    near = lax.div(row_index, 2) == lax.div(col_index, 2)
    even = [jnp.where(near, early[0], early[1]), jnp.where(near, early[1], early[0])]
    odd = [jnp.where(near, early[2], three), jnp.where(near, three, early[2])]
    for i in range(2):
        away[i] = jnp.where(keeps_even, odd[i], even[i])
        keep[i] = jnp.where(keeps_even, even[i], odd[i])


def sum_kernel(keep, came, own, other_low, other_top):
    own[...] = keep[0] + came[0]
    other_low[...] = keep[1, LOW] + came[1, LOW]
    other_top[...] = keep[1, TOP] + came[1, TOP]


def first_kernel(side, one, two, factor, low):
    low[...] = side[LOW, :] - (one[LOW, :] + two[...])

    @pl.when(lax.axis_index("row") == 0)
    def _():
        low[...] = product(factor[LOW, columns(0)], wide(low[...]))


def top_kernel(side, one, two, factor, low, top):
    top[...] = side[TOP, :] - (one[TOP, :] + two[...])

    @pl.when(lax.axis_index("row") == 0)
    def _():
        top[...] = top[...] - product(factor[TOP, columns(0)], wide(low[...]))


def second_kernel(solved, low_in, factor, low):
    @pl.when(lax.axis_index("row") == 1)
    def _():
        value = low_in[...] - product(factor[LOW, columns(0)], wide(solved[...]))
        low[LOW, :] = solved[...]
        low[TOP, :] = product(factor[LOW, columns(1)], wide(value))


def five_kernel(solved, top_in, factor, top):
    @pl.when(lax.axis_index("row") == 1)
    def _():
        value = top_in[...] - product(factor[TOP, columns(0)], wide(solved[LOW, :]))
        top[...] = value - product(factor[TOP, columns(1)], wide(solved[TOP, :]))


def last_kernel(low, low1, low2, top2, last3, last7, block4, block5, out):
    row_index = lax.axis_index("row")

    @pl.when(row_index == 0)
    def _():
        out[LOW, :] = low[...]
        out[TOP, :] = block4[...]

    @pl.when(row_index == 1)
    def _():
        out[LOW, :] = low1[TOP, :]
        out[TOP, :] = block5[...]

    @pl.when(row_index == 2)
    def _():
        out[LOW, :] = low2[...]
        out[TOP, :] = top2[...]

    @pl.when(row_index == 3)
    def _():
        out[LOW, :] = last3[...]
        out[TOP, :] = last7[...]


def halves():
    core = lax.axis_index("col") % 2
    own = pl.ds(pl.multiple_of(core * HALF, HALF), HALF)
    other = pl.ds(pl.multiple_of((1 - core) * HALF, HALF), HALF)
    return own, other


def stacked(ref, j):
    return jnp.concatenate([ref[j * BLOCK : j * BLOCK + HALF, :], ref[j * BLOCK + HALF : (j + 1) * BLOCK, :]], 1)


def join_kernel(*refs):
    out, at = refs[-1], 0
    for ref in refs[:-1]:
        out[at : at + ref.shape[0], :] = ref[...]
        at += ref.shape[0]


def third_kernel(first, second, low2, top2, factor, mine, theirs, block2, block3, change4, change5, change6, change7, value):
    @pl.when(lax.axis_index("row") == 2)
    def _():
        own, other = halves()
        sides = ((own, mine), (other, theirs))
        pairs = [wide(second[LOW, :]), wide(second[TOP, :])]
        start = low2[...]
        for k in range(2):
            start = start - product(factor[LOW, columns(k)], pairs[k])
        block2[...] = product(factor[LOW, columns(2)], wide(start))
        pairs.append(wide(block2[...]))
        for rows, tiles in sides:
            start = first[rows, :]
            for k in range(3):
                start = start - product(stacked(tiles, k), pairs[k])
            value[rows, :] = start
        pair = wide(value[...])
        for rows, tiles in sides:
            block3[rows, :] = product(stacked(tiles, 3), pair)
        pairs.append(wide(block3[...]))
        for rows, tiles in sides:
            change4[rows, :] = sum(product(stacked(tiles, 10 + k - 1), pairs[k]) for k in range(1, 4))
            change5[rows, :] = sum(product(stacked(tiles, 14 + k - 2), pairs[k]) for k in range(2, 4))
            change7[rows, :] = sum(product(stacked(tiles, 4 + k), pairs[k]) for k in range(4))
        change6[...] = top2[...] - sum(product(factor[TOP, columns(k)], pairs[k]) for k in range(4))


def fourth_kernel(
    value4, value5, top3, change4, change5, value6, change7, factor, mine, theirs, kept, block4, block5, sent
):
    @pl.when(lax.axis_index("row") == 2)
    def _():
        own, other = halves()
        sides = ((own, mine), (other, theirs))
        pair = wide(value4[...] - change4[...])
        for rows, tiles in sides:
            block4[rows, :] = product(stacked(tiles, 13), pair)
        four = wide(block4[...])
        for rows, tiles in sides:
            sent[rows, :] = value5[rows, :] - change5[rows, :] - product(stacked(tiles, 16), four)
        pair = wide(sent[...])
        for rows, tiles in sides:
            block5[rows, :] = product(stacked(tiles, 17), pair)
        five = wide(block5[...])
        kept[...] = value6[...] - product(factor[TOP, columns(4)], four) - product(factor[TOP, columns(5)], five)
        for rows, tiles in sides:
            start = top3[rows, :] - change7[rows, :] - product(stacked(tiles, 8), four)
            sent[rows, :] = start - product(stacked(tiles, 9), five)


def line4(right_side, prev_factor, prev_solution, window_factor):
    def move(x, *pairs):
        return lax.ppermute(x, "row", list(pairs))

    def swap(x):
        return lax.ppermute(x, "col", [(0, 1), (1, 0), (2, 3), (3, 2)])

    def cross(x):
        return lax.ppermute(x, "col", [(0, 2), (2, 0), (1, 3), (3, 1)])

    def edges(x):
        return move(x, (0, 1), (1, 0), (2, 3), (3, 2))

    def middle(x):
        return move(x, (1, 2), (2, 1))

    size, rows, tall = (BLOCK, WIDTH), (2 * BLOCK, WIDTH), prev_solution.shape
    dma = pltpu.SemaphoreType.DMA

    edge1 = edges(prev_solution)
    middle3 = middle(prev_solution)
    (carried,) = call(inject_kernel, [tall], [dma((8,))], [pltpu.VMEM, pltpu.HBM], aliases={0: 0})(
        middle3, window_factor
    )
    edge2 = edges(carried)
    middle2 = middle(edge1)
    past, factor, side, send5, send7, send8 = call(
        load_kernel,
        [prev_factor.shape, window_factor.shape, rows, tall, tall, rows],
        [dma((23,))],
        pltpu.HBM,
    )(after(prev_factor, carried, edge1), window_factor, right_side)
    (carried,) = call(inject_seven_kernel, [tall], aliases={0: 0})(middle2, send7)
    middle2 = carried
    edge3 = edges(carried)

    (early,) = call(early_kernel, [(3, *rows)])(past, prev_solution, edge1, edge2, middle2)
    (send45,) = call(join_kernel, [(2 * tall[0], WIDTH)])(after(edge2, early), send5)
    mine45 = move(send45, (1, 2))
    away, keep = call(late_kernel, [(2, *rows)] * 2)(past, early, edge3, middle3)
    one, other_low, other_top = call(sum_kernel, [rows, size, size])(keep, swap(away))
    two_low, two_top = cross(other_low), cross(other_top)
    own8 = move(after(send8, one), (3, 2))
    (low,) = call(first_kernel, [size])(side, one, two_low, factor)
    first = move(low, (0, 1), (3, 2))
    (top,) = call(top_kernel, [size])(side, one, two_top, factor, low)
    value4 = move(top, (0, 2))
    top3 = move(top, (3, 2))
    (mine,) = call(join_kernel, [(4 * tall[0] + rows[0], WIDTH)])(edge2, edge3, own8, after(mine45, first, top))
    theirs = swap(mine)
    (low1,) = call(second_kernel, [rows])(first, after(low, top), factor)
    second = move(low1, (1, 2))
    (top1,) = call(five_kernel, [size])(low1, top, factor)
    value5 = move(top1, (1, 2))
    block2, block3, change4, change5, value6, change7 = call(third_kernel, [size] * 6, [pltpu.VMEM(size, jnp.float32)])(
        first, second, low, top, factor, mine, theirs
    )
    last3 = move(block3, (2, 3))
    kept, block4, block5, sent = call(fourth_kernel, [size] * 4)(
        value4, value5, top3, change4, change5, value6, change7, factor, mine, theirs
    )
    last7 = move(sent, (2, 3))
    block5 = move(block5, (2, 1))
    block4 = move(block4, (2, 0))
    return call(last_kernel, [rows], inside=False)(
        low, low1, block2, kept, last3, last7, block4, block5
    )[0]


def body(right_side, prev_factor, prev_solution, window_factor):
    blocks = window_factor.shape[1] // STEPS
    slots = right_side.shape[0] // blocks
    if lax.axis_size("row") == 4 and lax.axis_size("col") == 4 and slots == 2:
        return line4(right_side, prev_factor, prev_solution, window_factor)
    return general(right_side, prev_factor, prev_solution, window_factor)


def solution(mesh):
    in_specs = (
        P(("groups", "row"), None),
        P(("groups", "row"), "col"),
        P(("groups", "col"), "row"),
        P(("groups", "row"), None),
    )
    out_specs = P(("groups", "row"), "col")
    return jax.shard_map(body, mesh=mesh, in_specs=in_specs, out_specs=out_specs, check_vma=False)
```

```python
import jax
import jax.numpy as jnp
from jax import lax
from jax.experimental import pallas as pl
from jax.experimental.pallas import tpu as pltpu
from jax.sharding import PartitionSpec as P

NRHS = 512
STEPS = 6
HIGH = lax.Precision.HIGH


def mul(a, b):
    return jnp.dot(a, b, precision=HIGH, preferred_element_type=jnp.float32)


def general(right_side, prev_factor, prev_solution, window_factor):
    row_count = lax.axis_size("row")
    row_index = lax.axis_index("row")
    col_count = lax.axis_size("col")
    col_index = lax.axis_index("col")
    blocks = window_factor.shape[1] // STEPS
    slots = right_side.shape[0] // blocks
    width = NRHS // col_count
    partial_value = mul(prev_factor, lax.all_gather(prev_solution, "row", axis=1, tiled=True))
    prior = lax.psum_scatter(partial_value, "col", scatter_dimension=1, tiled=True)
    mine = lax.dynamic_slice_in_dim(right_side, col_index * width, width, 1)
    resid = (mine - prior).reshape(slots, blocks, width)
    tiles = window_factor.reshape(slots, blocks, STEPS, blocks)
    order = jnp.arange(slots, dtype=jnp.int32) * row_count + row_index
    for step in range(STEPS):
        root = step % row_count
        solved = mul(tiles[step // row_count, :, step, :], resid[step // row_count])
        solved = lax.psum(jnp.where(row_index == root, solved, jnp.zeros_like(solved)), "row")
        update = jnp.einsum("sij,jn->sin", tiles[:, :, step, :], solved, precision=HIGH)
        resid = jnp.where((order > step)[:, None, None], resid - update, resid)
        resid = jnp.where((order == step)[:, None, None], solved[None], resid)
    return resid.reshape(slots * blocks, width)


BLOCK = 256
HALF = BLOCK // 2
WIDTH = 128
VMEM_SPEC = pl.BlockSpec(memory_space=pltpu.VMEM)


def after(x, *earlier):
    return lax.optimization_barrier((x, *earlier))[0]


def split(x):
    high = x.astype(jnp.bfloat16)
    return high, (x - high.astype(jnp.float32)).astype(jnp.bfloat16)


def wide(x):
    return jnp.concatenate(split(x), 1)


def product(tile, pair):
    high, low = split(tile)
    both = jnp.dot(high, pair, preferred_element_type=jnp.float32)
    both = both + jnp.dot(low, pair, preferred_element_type=jnp.float32)
    return both[:, :WIDTH] + both[:, WIDTH:]


def columns(k):
    return slice(k * BLOCK, (k + 1) * BLOCK)


LOW, TOP = slice(0, BLOCK), slice(BLOCK, 2 * BLOCK)


def call(kernel, shapes, scratch=(), space=pltpu.VMEM, inside=True, aliases={}):
    def run(*args):
        spaces = space if isinstance(space, list) else [space] * len(args)
        return pl.pallas_call(
            kernel,
            out_shape=[(pltpu.VMEM if inside else jax.ShapeDtypeStruct)(s, jnp.float32) for s in shapes],
            in_specs=[pl.BlockSpec(memory_space=m) for m in spaces],
            out_specs=[VMEM_SPEC] * len(shapes),
            scratch_shapes=list(scratch),
            input_output_aliases=aliases,
            compiler_params=pltpu.CompilerParams(vmem_limit_bytes=32 * 1024 * 1024),
        )(*[pltpu.with_memory_space_constraint(a, m) for a, m in zip(args, spaces)])

    return run


def sent_rows():
    core = lax.axis_index("col") % 2
    low = pl.ds(pl.multiple_of(core * HALF, HALF), HALF)
    return low, pl.ds(pl.multiple_of(BLOCK + core * HALF, HALF), HALF)


def copy_all(pairs, sem):
    copies = [pltpu.make_async_copy(s, d, sem.at[i]) for i, (s, d) in enumerate(pairs)]
    for copy in copies:
        copy.start()
    for copy in copies:
        copy.wait()


def stack_copies(source, rows, start, out, count=8):
    return [
        (source.at[rows, pl.ds(start + j * HALF, HALF)], out.at[slice(j * HALF, (j + 1) * HALF), :])
        for j in range(count)
    ]


def inject_kernel(x_in, factor, x, sem):
    low, top = sent_rows()

    @pl.when(lax.axis_index("row") == 0)
    def _():
        copy_all(stack_copies(factor, top, BLOCK, x), sem)

    @pl.when(lax.axis_index("row") == 3)
    def _():
        copy_all(stack_copies(factor, low, 0, x), sem)


def inject_seven_kernel(x_in, seven, x):
    @pl.when(lax.axis_index("row") == 3)
    def _():
        x[...] = seven[...]


def load_kernel(past, factor, side, past_out, factor_out, side_out, five, seven, eight, sem):
    _, top = sent_rows()
    mine = pl.ds(pl.multiple_of(lax.axis_index("col") * WIDTH, WIDTH), WIDTH)
    copy_all(
        stack_copies(factor, top, 0, seven)
        + [
            (past, past_out),
            (factor, factor_out),
            (side.at[:, mine], side_out),
        ]
        + stack_copies(factor, top, 2 * BLOCK, five)
        + stack_copies(factor, top, 4 * BLOCK, eight, 4),
        sem,
    )


def spread(factor, *parts):
    high, low = split(factor)
    pair = jnp.concatenate([wide(x) for x in parts], 1)
    both = jnp.dot(high, pair, preferred_element_type=jnp.float32)
    both = both + jnp.dot(low, pair, preferred_element_type=jnp.float32)
    lanes = [both[:, i * WIDTH : (i + 1) * WIDTH] for i in range(2 * len(parts))]
    return [lanes[2 * i] + lanes[2 * i + 1] for i in range(len(parts))]


def at_end():
    row_index = lax.axis_index("row")
    return jnp.logical_or(row_index == 0, row_index == 3)


def early_kernel(past, own, edge1, edge2, middle2, early):
    got = spread(past[...], own[...], jnp.where(at_end(), edge2[...], middle2[...]), edge1[...])
    for i in range(3):
        early[i] = got[i]


def late_kernel(past, early, edge3, middle3, away, keep):
    row_index, col_index = lax.axis_index("row"), lax.axis_index("col")
    keeps_even = lax.rem(col_index, 2) == lax.rem(row_index, 2)
    (three,) = spread(past[...], jnp.where(at_end(), edge3[...], middle3[...]))
    near = lax.div(row_index, 2) == lax.div(col_index, 2)
    even = [jnp.where(near, early[0], early[1]), jnp.where(near, early[1], early[0])]
    odd = [jnp.where(near, early[2], three), jnp.where(near, three, early[2])]
    for i in range(2):
        away[i] = jnp.where(keeps_even, odd[i], even[i])
        keep[i] = jnp.where(keeps_even, even[i], odd[i])


def sum_kernel(keep, came, own, other_low, other_top):
    own[...] = keep[0] + came[0]
    other_low[...] = keep[1, LOW] + came[1, LOW]
    other_top[...] = keep[1, TOP] + came[1, TOP]


def first_kernel(side, one, two, factor, low):
    low[...] = side[LOW, :] - (one[LOW, :] + two[...])

    @pl.when(lax.axis_index("row") == 0)
    def _():
        low[...] = product(factor[LOW, columns(0)], wide(low[...]))


def top_kernel(side, one, two, factor, low, top):
    top[...] = side[TOP, :] - (one[TOP, :] + two[...])

    @pl.when(lax.axis_index("row") == 0)
    def _():
        top[...] = top[...] - product(factor[TOP, columns(0)], wide(low[...]))


def second_kernel(solved, low_in, factor, low):
    @pl.when(lax.axis_index("row") == 1)
    def _():
        value = low_in[...] - product(factor[LOW, columns(0)], wide(solved[...]))
        low[...] = product(factor[LOW, columns(1)], wide(value))


def five_kernel(zero, one, top_in, factor, top):
    @pl.when(lax.axis_index("row") == 1)
    def _():
        value = top_in[...] - product(factor[TOP, columns(0)], wide(zero[...]))
        top[...] = value - product(factor[TOP, columns(1)], wide(one[...]))


def last_kernel(block4, block5, last3, last7, low, low1, low2, top2, out):
    row_index = lax.axis_index("row")

    @pl.when(row_index == 0)
    def _():
        out[LOW, :] = low[...]
        out[TOP, :] = block4[...]

    @pl.when(row_index == 1)
    def _():
        out[LOW, :] = low1[...]
        out[TOP, :] = block5[...]

    @pl.when(row_index == 2)
    def _():
        out[LOW, :] = low2[...]
        out[TOP, :] = top2[...]

    @pl.when(row_index == 3)
    def _():
        out[LOW, :] = last3[...]
        out[TOP, :] = last7[...]


def halves():
    core = lax.axis_index("col") % 2
    own = pl.ds(pl.multiple_of(core * HALF, HALF), HALF)
    other = pl.ds(pl.multiple_of((1 - core) * HALF, HALF), HALF)
    return own, other


def stacked(ref, j):
    return jnp.concatenate([ref[j * BLOCK : j * BLOCK + HALF, :], ref[j * BLOCK + HALF : (j + 1) * BLOCK, :]], 1)


def join_kernel(*refs):
    out, at = refs[-1], 0
    for ref in refs[:-1]:
        out[at : at + ref.shape[0], :] = ref[...]
        at += ref.shape[0]


def third_kernel(first, zero, second, low2, top2, factor, mine, theirs, block2, block3, change4, change5, change6, change7, value):
    @pl.when(lax.axis_index("row") == 2)
    def _():
        own, other = halves()
        sides = ((own, mine), (other, theirs))
        pairs = [wide(zero[...]), wide(second[...])]
        start = low2[...]
        for k in range(2):
            start = start - product(factor[LOW, columns(k)], pairs[k])
        block2[...] = product(factor[LOW, columns(2)], wide(start))
        pairs.append(wide(block2[...]))
        for rows, tiles in sides:
            start = first[rows, :]
            for k in range(3):
                start = start - product(stacked(tiles, k), pairs[k])
            value[rows, :] = start
        pair = wide(value[...])
        for rows, tiles in sides:
            block3[rows, :] = product(stacked(tiles, 3), pair)
        pairs.append(wide(block3[...]))
        for rows, tiles in sides:
            change4[rows, :] = sum(product(stacked(tiles, 10 + k - 1), pairs[k]) for k in range(1, 4))
            change5[rows, :] = sum(product(stacked(tiles, 14 + k - 2), pairs[k]) for k in range(2, 4))
            change7[rows, :] = sum(product(stacked(tiles, 4 + k), pairs[k]) for k in range(4))
        change6[...] = top2[...] - sum(product(factor[TOP, columns(k)], pairs[k]) for k in range(4))


def fourth_kernel(
    change4, change5, value6, change7, factor, mine, theirs, value5, value4, top3, kept, block4, block5, sent
):
    @pl.when(lax.axis_index("row") == 2)
    def _():
        own, other = halves()
        sides = ((own, mine), (other, theirs))
        pair = wide(value4[...] - change4[...])
        for rows, tiles in sides:
            block4[rows, :] = product(stacked(tiles, 13), pair)
        four = wide(block4[...])
        for rows, tiles in sides:
            sent[rows, :] = value5[rows, :] - change5[rows, :] - product(stacked(tiles, 16), four)
        pair = wide(sent[...])
        for rows, tiles in sides:
            block5[rows, :] = product(stacked(tiles, 17), pair)
        five = wide(block5[...])
        kept[...] = value6[...] - product(factor[TOP, columns(4)], four) - product(factor[TOP, columns(5)], five)
        for rows, tiles in sides:
            start = top3[rows, :] - change7[rows, :] - product(stacked(tiles, 8), four)
            sent[rows, :] = start - product(stacked(tiles, 9), five)


def line4(right_side, prev_factor, prev_solution, window_factor):
    def move(x, *pairs):
        return lax.ppermute(x, "row", list(pairs))

    def swap(x):
        return lax.ppermute(x, "col", [(0, 1), (1, 0), (2, 3), (3, 2)])

    def cross(x):
        return lax.ppermute(x, "col", [(0, 2), (2, 0), (1, 3), (3, 1)])

    def edges(x):
        return move(x, (0, 1), (1, 0), (2, 3), (3, 2))

    def middle(x):
        return move(x, (1, 2), (2, 1))

    size, rows, tall = (BLOCK, WIDTH), (2 * BLOCK, WIDTH), prev_solution.shape
    dma = pltpu.SemaphoreType.DMA

    edge1 = edges(prev_solution)
    middle3 = middle(prev_solution)
    (carried,) = call(inject_kernel, [tall], [dma((8,))], [pltpu.VMEM, pltpu.HBM], aliases={0: 0})(
        middle3, window_factor
    )
    edge2 = edges(carried)
    middle2 = middle(edge1)
    past, factor, side, send5, send7, send8 = call(
        load_kernel,
        [prev_factor.shape, window_factor.shape, rows, tall, tall, rows],
        [dma((23,))],
        pltpu.HBM,
    )(after(prev_factor, carried, edge1), window_factor, right_side)
    (carried,) = call(inject_seven_kernel, [tall], aliases={0: 0})(middle2, send7)
    middle2 = carried
    edge3 = edges(carried)

    (early,) = call(early_kernel, [(3, *rows)])(past, prev_solution, edge1, edge2, middle2)
    (send45,) = call(join_kernel, [(2 * tall[0], WIDTH)])(after(edge2, early), send5)
    mine45 = move(send45, (1, 2))
    away, keep = call(late_kernel, [(2, *rows)] * 2)(past, early, edge3, middle3)
    one, other_low, other_top = call(sum_kernel, [rows, size, size])(keep, swap(away))
    two_low, two_top = cross(other_low), cross(other_top)
    own8 = move(after(send8, one), (3, 2))
    (low,) = call(first_kernel, [size])(side, one, two_low, factor)
    first = move(low, (0, 1), (3, 2))
    zero = move(low, (0, 2))
    (top,) = call(top_kernel, [size])(side, one, two_top, factor, low)
    value4 = move(top, (0, 2))
    top3 = move(top, (3, 2))
    (mine,) = call(join_kernel, [(4 * tall[0] + rows[0], WIDTH)])(edge2, edge3, own8, after(mine45, first, zero, top))
    theirs = swap(mine)
    (low1,) = call(second_kernel, [size])(first, after(low, top), factor)
    second = move(low1, (1, 2))
    (top1,) = call(five_kernel, [size])(first, low1, top, factor)
    value5 = move(top1, (1, 2))
    block2, block3, change4, change5, value6, change7 = call(third_kernel, [size] * 6, [pltpu.VMEM(size, jnp.float32)])(
        first, zero, second, low, top, factor, mine, theirs
    )
    last3 = move(block3, (2, 3))
    kept, block4, block5, sent = call(fourth_kernel, [size] * 4)(
        change4, change5, value6, change7, factor, mine, theirs, value5, value4, top3
    )
    last7 = move(sent, (2, 3))
    block5 = move(block5, (2, 1))
    block4 = move(block4, (2, 0))
    return call(last_kernel, [rows], inside=False)(
        block4, block5, last3, last7, low, low1, block2, kept
    )[0]


def body(right_side, prev_factor, prev_solution, window_factor):
    blocks = window_factor.shape[1] // STEPS
    slots = right_side.shape[0] // blocks
    if lax.axis_size("row") == 4 and lax.axis_size("col") == 4 and slots == 2:
        return line4(right_side, prev_factor, prev_solution, window_factor)
    return general(right_side, prev_factor, prev_solution, window_factor)


def solution(mesh):
    in_specs = (
        P(("groups", "row"), None),
        P(("groups", "row"), "col"),
        P(("groups", "col"), "row"),
        P(("groups", "row"), None),
    )
    out_specs = P(("groups", "row"), "col")
    return jax.shard_map(body, mesh=mesh, in_specs=in_specs, out_specs=out_specs, check_vma=False)
```

```python
import jax
import jax.numpy as jnp
from jax import lax
from jax.experimental import pallas as pl
from jax.experimental.pallas import tpu as pltpu
from jax.sharding import PartitionSpec as P

NRHS = 512
STEPS = 6
HIGH = lax.Precision.HIGH


def mul(a, b):
    return jnp.dot(a, b, precision=HIGH, preferred_element_type=jnp.float32)


def general(right_side, prev_factor, prev_solution, window_factor):
    row_count = lax.axis_size("row")
    row_index = lax.axis_index("row")
    col_count = lax.axis_size("col")
    col_index = lax.axis_index("col")
    blocks = window_factor.shape[1] // STEPS
    slots = right_side.shape[0] // blocks
    width = NRHS // col_count
    partial_value = mul(prev_factor, lax.all_gather(prev_solution, "row", axis=1, tiled=True))
    prior = lax.psum_scatter(partial_value, "col", scatter_dimension=1, tiled=True)
    mine = lax.dynamic_slice_in_dim(right_side, col_index * width, width, 1)
    resid = (mine - prior).reshape(slots, blocks, width)
    tiles = window_factor.reshape(slots, blocks, STEPS, blocks)
    order = jnp.arange(slots, dtype=jnp.int32) * row_count + row_index
    for step in range(STEPS):
        root = step % row_count
        solved = mul(tiles[step // row_count, :, step, :], resid[step // row_count])
        solved = lax.psum(jnp.where(row_index == root, solved, jnp.zeros_like(solved)), "row")
        update = jnp.einsum("sij,jn->sin", tiles[:, :, step, :], solved, precision=HIGH)
        resid = jnp.where((order > step)[:, None, None], resid - update, resid)
        resid = jnp.where((order == step)[:, None, None], solved[None], resid)
    return resid.reshape(slots * blocks, width)


BLOCK = 256
HALF = BLOCK // 2
WIDTH = 128
VMEM_SPEC = pl.BlockSpec(memory_space=pltpu.VMEM)


def after(x, *earlier):
    return lax.optimization_barrier((x, *earlier))[0]


def split(x):
    high = x.astype(jnp.bfloat16)
    return high, (x - high.astype(jnp.float32)).astype(jnp.bfloat16)


def wide(x):
    return jnp.concatenate(split(x), 1)


def product(tile, pair):
    high, low = split(tile)
    both = jnp.dot(high, pair, preferred_element_type=jnp.float32)
    both = both + jnp.dot(low, pair, preferred_element_type=jnp.float32)
    return both[:, :WIDTH] + both[:, WIDTH:]


def columns(k):
    return slice(k * BLOCK, (k + 1) * BLOCK)


LOW, TOP = slice(0, BLOCK), slice(BLOCK, 2 * BLOCK)


def call(kernel, shapes, scratch=(), space=pltpu.VMEM, inside=True, aliases={}):
    def run(*args):
        spaces = space if isinstance(space, list) else [space] * len(args)
        return pl.pallas_call(
            kernel,
            out_shape=[(pltpu.VMEM if inside else jax.ShapeDtypeStruct)(s, jnp.float32) for s in shapes],
            in_specs=[pl.BlockSpec(memory_space=m) for m in spaces],
            out_specs=[VMEM_SPEC] * len(shapes),
            scratch_shapes=list(scratch),
            input_output_aliases=aliases,
            compiler_params=pltpu.CompilerParams(vmem_limit_bytes=32 * 1024 * 1024),
        )(*[pltpu.with_memory_space_constraint(a, m) for a, m in zip(args, spaces)])

    return run


def sent_rows():
    core = lax.axis_index("col") % 2
    low = pl.ds(pl.multiple_of(core * HALF, HALF), HALF)
    return low, pl.ds(pl.multiple_of(BLOCK + core * HALF, HALF), HALF)


def copy_all(pairs, sem):
    copies = [pltpu.make_async_copy(s, d, sem.at[i]) for i, (s, d) in enumerate(pairs)]
    for copy in copies:
        copy.start()
    for copy in copies:
        copy.wait()


def stack_copies(source, rows, start, out, count=8):
    return [
        (source.at[rows, pl.ds(start + j * HALF, HALF)], out.at[slice(j * HALF, (j + 1) * HALF), :])
        for j in range(count)
    ]


def inject_kernel(x_in, factor, x, sem):
    low, top = sent_rows()

    @pl.when(lax.axis_index("row") == 0)
    def _():
        copy_all(stack_copies(factor, top, BLOCK, x), sem)

    @pl.when(lax.axis_index("row") == 3)
    def _():
        copy_all(stack_copies(factor, low, 0, x), sem)


def inject_seven_kernel(x_in, seven, x):
    @pl.when(lax.axis_index("row") == 3)
    def _():
        x[...] = seven[...]


def load_kernel(past, factor, side, past_out, factor_out, side_out, five, seven, eight, sem):
    _, top = sent_rows()
    mine = pl.ds(pl.multiple_of(lax.axis_index("col") * WIDTH, WIDTH), WIDTH)
    copy_all(
        stack_copies(factor, top, 0, seven)
        + [
            (past, past_out),
            (factor, factor_out),
            (side.at[:, mine], side_out),
        ]
        + stack_copies(factor, top, 2 * BLOCK, five)
        + stack_copies(factor, top, 4 * BLOCK, eight, 4),
        sem,
    )


def spread(factor, *parts):
    high, low = split(factor)
    pair = jnp.concatenate([wide(x) for x in parts], 1)
    both = jnp.dot(high, pair, preferred_element_type=jnp.float32)
    both = both + jnp.dot(low, pair, preferred_element_type=jnp.float32)
    lanes = [both[:, i * WIDTH : (i + 1) * WIDTH] for i in range(2 * len(parts))]
    return [lanes[2 * i] + lanes[2 * i + 1] for i in range(len(parts))]


def at_end():
    row_index = lax.axis_index("row")
    return jnp.logical_or(row_index == 0, row_index == 3)


def keeps_even():
    return lax.rem(lax.axis_index("col"), 2) == lax.rem(lax.axis_index("row"), 2)


def early_kernel(past, own, edge1, edge2, middle2, early, away):
    got = spread(past[...], own[...], jnp.where(at_end(), edge2[...], middle2[...]), edge1[...])
    for i in range(3):
        early[i] = got[i]
    away[...] = jnp.where(keeps_even(), got[2], got[0])


def late_kernel(past, early, came, edge3, middle3, away, keep, total):
    even = keeps_even()
    (three,) = spread(past[...], jnp.where(at_end(), edge3[...], middle3[...]))
    away[...] = jnp.where(even, three, early[1])
    keep[...] = jnp.where(even, early[1], three)
    total[...] = jnp.where(even, early[0], early[2]) + came[...]


def sum_kernel(keep, came, total, own, other_low, other_top):
    near = lax.div(lax.axis_index("row"), 2) == lax.div(lax.axis_index("col"), 2)
    late = keep[...] + came[...]
    own[...] = jnp.where(near, total[...], late)
    other = jnp.where(near, late, total[...])
    other_low[...] = other[LOW, :]
    other_top[...] = other[TOP, :]


def first_kernel(side, one, two, factor, low):
    low[...] = side[LOW, :] - (one[LOW, :] + two[...])

    @pl.when(lax.axis_index("row") == 0)
    def _():
        low[...] = product(factor[LOW, columns(0)], wide(low[...]))


def top_kernel(side, one, two, factor, low, top):
    top[...] = side[TOP, :] - (one[TOP, :] + two[...])

    @pl.when(lax.axis_index("row") == 0)
    def _():
        top[...] = top[...] - product(factor[TOP, columns(0)], wide(low[...]))


def second_kernel(solved, low_in, factor, low):
    @pl.when(lax.axis_index("row") == 1)
    def _():
        value = low_in[...] - product(factor[LOW, columns(0)], wide(solved[...]))
        low[...] = product(factor[LOW, columns(1)], wide(value))


def five_kernel(zero, one, top_in, factor, top):
    @pl.when(lax.axis_index("row") == 1)
    def _():
        value = top_in[...] - product(factor[TOP, columns(0)], wide(zero[...]))
        top[...] = value - product(factor[TOP, columns(1)], wide(one[...]))


def last_kernel(block4, block5, last3, last7, low, low1, low2, top2, out):
    row_index = lax.axis_index("row")

    @pl.when(row_index == 0)
    def _():
        out[LOW, :] = low[...]
        out[TOP, :] = block4[...]

    @pl.when(row_index == 1)
    def _():
        out[LOW, :] = low1[...]
        out[TOP, :] = block5[...]

    @pl.when(row_index == 2)
    def _():
        out[LOW, :] = low2[...]
        out[TOP, :] = top2[...]

    @pl.when(row_index == 3)
    def _():
        out[LOW, :] = last3[...]
        out[TOP, :] = last7[...]


def halves():
    core = lax.axis_index("col") % 2
    own = pl.ds(pl.multiple_of(core * HALF, HALF), HALF)
    other = pl.ds(pl.multiple_of((1 - core) * HALF, HALF), HALF)
    return own, other


def stacked(ref, j):
    return jnp.concatenate([ref[j * BLOCK : j * BLOCK + HALF, :], ref[j * BLOCK + HALF : (j + 1) * BLOCK, :]], 1)


def join_kernel(*refs):
    out, at = refs[-1], 0
    for ref in refs[:-1]:
        out[at : at + ref.shape[0], :] = ref[...]
        at += ref.shape[0]


def zero_kernel(zero, first, low2, top2, factor, mine, theirs, state2, state3, state6, change7):
    @pl.when(lax.axis_index("row") == 2)
    def _():
        own, other = halves()
        pair = wide(zero[...])
        state2[...] = low2[...] - product(factor[LOW, columns(0)], pair)
        state6[...] = top2[...] - product(factor[TOP, columns(0)], pair)
        for rows, tiles in ((own, mine), (other, theirs)):
            state3[rows, :] = first[rows, :] - product(stacked(tiles, 0), pair)
            change7[rows, :] = product(stacked(tiles, 4), pair)


def third_kernel(
    second, state2, state3, state6, state7, factor, mine, theirs,
    block2, block3, change4, change5, value6, change7, value,
):
    @pl.when(lax.axis_index("row") == 2)
    def _():
        own, other = halves()
        sides = ((own, mine), (other, theirs))
        pairs = {1: wide(second[...])}
        block2[...] = product(
            factor[LOW, columns(2)], wide(state2[...] - product(factor[LOW, columns(1)], pairs[1]))
        )
        pairs[2] = wide(block2[...])
        for rows, tiles in sides:
            start = state3[rows, :] - product(stacked(tiles, 1), pairs[1])
            value[rows, :] = start - product(stacked(tiles, 2), pairs[2])
        pair = wide(value[...])
        for rows, tiles in sides:
            block3[rows, :] = product(stacked(tiles, 3), pair)
        pairs[3] = wide(block3[...])
        for rows, tiles in sides:
            change4[rows, :] = sum(product(stacked(tiles, 10 + k - 1), pairs[k]) for k in range(1, 4))
            change5[rows, :] = sum(product(stacked(tiles, 14 + k - 2), pairs[k]) for k in range(2, 4))
            change7[rows, :] = state7[rows, :] + sum(product(stacked(tiles, 4 + k), pairs[k]) for k in range(1, 4))
        value6[...] = state6[...] - sum(product(factor[TOP, columns(k)], pairs[k]) for k in range(1, 4))


def fourth_kernel(
    change4, change5, value6, change7, factor, mine, theirs, value5, value4, top3, kept, block4, block5, sent
):
    @pl.when(lax.axis_index("row") == 2)
    def _():
        own, other = halves()
        sides = ((own, mine), (other, theirs))
        pair = wide(value4[...] - change4[...])
        for rows, tiles in sides:
            block4[rows, :] = product(stacked(tiles, 13), pair)
        four = wide(block4[...])
        for rows, tiles in sides:
            sent[rows, :] = value5[rows, :] - change5[rows, :] - product(stacked(tiles, 16), four)
        pair = wide(sent[...])
        for rows, tiles in sides:
            block5[rows, :] = product(stacked(tiles, 17), pair)
        five = wide(block5[...])
        kept[...] = value6[...] - product(factor[TOP, columns(4)], four) - product(factor[TOP, columns(5)], five)
        for rows, tiles in sides:
            start = top3[rows, :] - change7[rows, :] - product(stacked(tiles, 8), four)
            sent[rows, :] = start - product(stacked(tiles, 9), five)


def line4(right_side, prev_factor, prev_solution, window_factor):
    def move(x, *pairs):
        return lax.ppermute(x, "row", list(pairs))

    def swap(x):
        return lax.ppermute(x, "col", [(0, 1), (1, 0), (2, 3), (3, 2)])

    def cross(x):
        return lax.ppermute(x, "col", [(0, 2), (2, 0), (1, 3), (3, 1)])

    def edges(x):
        return move(x, (0, 1), (1, 0), (2, 3), (3, 2))

    def middle(x):
        return move(x, (1, 2), (2, 1))

    size, rows, tall = (BLOCK, WIDTH), (2 * BLOCK, WIDTH), prev_solution.shape
    dma = pltpu.SemaphoreType.DMA

    edge1 = edges(prev_solution)
    middle3 = middle(prev_solution)
    (carried,) = call(inject_kernel, [tall], [dma((8,))], [pltpu.VMEM, pltpu.HBM], aliases={0: 0})(
        middle3, window_factor
    )
    edge2 = edges(carried)
    middle2 = middle(edge1)
    past, factor, side, send5, send7, send8 = call(
        load_kernel,
        [prev_factor.shape, window_factor.shape, rows, tall, tall, rows],
        [dma((23,))],
        pltpu.HBM,
    )(after(prev_factor, carried, edge1), window_factor, right_side)
    (carried,) = call(inject_seven_kernel, [tall], aliases={0: 0})(middle2, send7)
    middle2 = carried
    edge3 = edges(carried)

    early, away = call(early_kernel, [(3, *rows), rows])(past, prev_solution, edge1, edge2, middle2)
    (send45,) = call(join_kernel, [(2 * tall[0], WIDTH)])(edge2, send5)
    mine45 = move(send45, (1, 2))
    away, keep, total = call(late_kernel, [rows] * 3)(past, early, swap(away), edge3, middle3)
    one, other_low, other_top = call(sum_kernel, [rows, size, size])(keep, swap(away), total)
    two_low, two_top = cross(other_low), cross(other_top)
    own8 = move(after(send8, one), (3, 2))
    (low,) = call(first_kernel, [size])(side, one, two_low, factor)
    first = move(low, (0, 1), (3, 2))
    zero = move(low, (0, 2))
    (top,) = call(top_kernel, [size])(side, one, two_top, factor, low)
    value4 = move(top, (0, 2))
    top3 = move(top, (3, 2))
    (mine,) = call(join_kernel, [(4 * tall[0] + rows[0], WIDTH)])(edge2, edge3, own8, after(mine45, first, zero, top))
    theirs = swap(mine)
    (low1,) = call(second_kernel, [size])(first, after(low, top), factor)
    second = move(low1, (1, 2))
    (top1,) = call(five_kernel, [size])(first, low1, top, factor)
    value5 = move(top1, (1, 2))
    states = call(zero_kernel, [size] * 4)(zero, first, low, top, factor, mine, theirs)
    block2, block3, change4, change5, value6, change7 = call(third_kernel, [size] * 6, [pltpu.VMEM(size, jnp.float32)])(
        second, *states, factor, mine, theirs
    )
    last3 = move(block3, (2, 3))
    kept, block4, block5, sent = call(fourth_kernel, [size] * 4)(
        change4, change5, value6, change7, factor, mine, theirs, value5, value4, top3
    )
    last7 = move(sent, (2, 3))
    block5 = move(block5, (2, 1))
    block4 = move(block4, (2, 0))
    return call(last_kernel, [rows], inside=False)(
        block4, block5, last3, last7, low, low1, block2, kept
    )[0]


def body(right_side, prev_factor, prev_solution, window_factor):
    blocks = window_factor.shape[1] // STEPS
    slots = right_side.shape[0] // blocks
    if lax.axis_size("row") == 4 and lax.axis_size("col") == 4 and slots == 2:
        return line4(right_side, prev_factor, prev_solution, window_factor)
    return general(right_side, prev_factor, prev_solution, window_factor)


def solution(mesh):
    in_specs = (
        P(("groups", "row"), None),
        P(("groups", "row"), "col"),
        P(("groups", "col"), "row"),
        P(("groups", "row"), None),
    )
    out_specs = P(("groups", "row"), "col")
    return jax.shard_map(body, mesh=mesh, in_specs=in_specs, out_specs=out_specs, check_vma=False)
```

```python
import jax
import jax.numpy as jnp
from jax import lax
from jax.experimental import pallas as pl
from jax.experimental.pallas import tpu as pltpu
from jax.sharding import PartitionSpec as P

NRHS = 512
STEPS = 6
HIGH = lax.Precision.HIGH


def mul(a, b):
    return jnp.dot(a, b, precision=HIGH, preferred_element_type=jnp.float32)


def general(right_side, prev_factor, prev_solution, window_factor):
    row_count = lax.axis_size("row")
    row_index = lax.axis_index("row")
    col_count = lax.axis_size("col")
    col_index = lax.axis_index("col")
    blocks = window_factor.shape[1] // STEPS
    slots = right_side.shape[0] // blocks
    width = NRHS // col_count
    partial_value = mul(prev_factor, lax.all_gather(prev_solution, "row", axis=1, tiled=True))
    prior = lax.psum_scatter(partial_value, "col", scatter_dimension=1, tiled=True)
    mine = lax.dynamic_slice_in_dim(right_side, col_index * width, width, 1)
    resid = (mine - prior).reshape(slots, blocks, width)
    tiles = window_factor.reshape(slots, blocks, STEPS, blocks)
    order = jnp.arange(slots, dtype=jnp.int32) * row_count + row_index
    for step in range(STEPS):
        root = step % row_count
        solved = mul(tiles[step // row_count, :, step, :], resid[step // row_count])
        solved = lax.psum(jnp.where(row_index == root, solved, jnp.zeros_like(solved)), "row")
        update = jnp.einsum("sij,jn->sin", tiles[:, :, step, :], solved, precision=HIGH)
        resid = jnp.where((order > step)[:, None, None], resid - update, resid)
        resid = jnp.where((order == step)[:, None, None], solved[None], resid)
    return resid.reshape(slots * blocks, width)


BLOCK = 256
HALF = BLOCK // 2
WIDTH = 128
VMEM_SPEC = pl.BlockSpec(memory_space=pltpu.VMEM)


def after(x, *earlier):
    return lax.optimization_barrier((x, *earlier))[0]


def split(x):
    high = x.astype(jnp.bfloat16)
    return high, (x - high.astype(jnp.float32)).astype(jnp.bfloat16)


def wide(x):
    return jnp.concatenate(split(x), 1)


def product(tile, pair):
    high, low = split(tile)
    both = jnp.dot(high, pair, preferred_element_type=jnp.float32)
    both = both + jnp.dot(low, pair, preferred_element_type=jnp.float32)
    return both[:, :WIDTH] + both[:, WIDTH:]


def square(one, two):
    high, low = split(one)
    pair = wide(two)
    both = jnp.dot(high, pair, preferred_element_type=jnp.float32)
    both = both + jnp.dot(low, pair, preferred_element_type=jnp.float32)
    return both[:, :BLOCK] + both[:, BLOCK:]


def columns(k):
    return slice(k * BLOCK, (k + 1) * BLOCK)


LOW, TOP = slice(0, BLOCK), slice(BLOCK, 2 * BLOCK)


def call(kernel, shapes, scratch=(), space=pltpu.VMEM, inside=True, aliases={}):
    def run(*args):
        spaces = space if isinstance(space, list) else [space] * len(args)
        return pl.pallas_call(
            kernel,
            out_shape=[(pltpu.VMEM if inside else jax.ShapeDtypeStruct)(s, jnp.float32) for s in shapes],
            in_specs=[pl.BlockSpec(memory_space=m) for m in spaces],
            out_specs=[VMEM_SPEC] * len(shapes),
            scratch_shapes=list(scratch),
            input_output_aliases=aliases,
            compiler_params=pltpu.CompilerParams(vmem_limit_bytes=32 * 1024 * 1024),
        )(*[pltpu.with_memory_space_constraint(a, m) for a, m in zip(args, spaces)])

    return run


def sent_rows():
    core = lax.axis_index("col") % 2
    low = pl.ds(pl.multiple_of(core * HALF, HALF), HALF)
    return low, pl.ds(pl.multiple_of(BLOCK + core * HALF, HALF), HALF)


def copy_all(pairs, sem):
    copies = [pltpu.make_async_copy(s, d, sem.at[i]) for i, (s, d) in enumerate(pairs)]
    for copy in copies:
        copy.start()
    for copy in copies:
        copy.wait()


def stack_copies(source, rows, start, out, count=8):
    return [
        (source.at[rows, pl.ds(start + j * HALF, HALF)], out.at[slice(j * HALF, (j + 1) * HALF), :])
        for j in range(count)
    ]


def inject_kernel(x_in, factor, x, sem):
    low, top = sent_rows()

    @pl.when(lax.axis_index("row") == 0)
    def _():
        copy_all(stack_copies(factor, top, BLOCK, x), sem)

    @pl.when(lax.axis_index("row") == 3)
    def _():
        copy_all(stack_copies(factor, low, 0, x), sem)


def inject_seven_kernel(x_in, seven, x):
    @pl.when(lax.axis_index("row") == 3)
    def _():
        x[...] = seven[...]


def load_kernel(past, factor, side, past_out, factor_out, side_out, five, seven, eight, sem):
    _, top = sent_rows()
    mine = pl.ds(pl.multiple_of(lax.axis_index("col") * WIDTH, WIDTH), WIDTH)
    copy_all(
        stack_copies(factor, top, 0, seven)
        + [
            (past, past_out),
            (factor, factor_out),
            (side.at[:, mine], side_out),
        ]
        + stack_copies(factor, top, 2 * BLOCK, five)
        + stack_copies(factor, top, 4 * BLOCK, eight, 4),
        sem,
    )


def spread(factor, *parts):
    high, low = split(factor)
    pair = jnp.concatenate([wide(x) for x in parts], 1)
    both = jnp.dot(high, pair, preferred_element_type=jnp.float32)
    both = both + jnp.dot(low, pair, preferred_element_type=jnp.float32)
    lanes = [both[:, i * WIDTH : (i + 1) * WIDTH] for i in range(2 * len(parts))]
    return [lanes[2 * i] + lanes[2 * i + 1] for i in range(len(parts))]


def at_end():
    row_index = lax.axis_index("row")
    return jnp.logical_or(row_index == 0, row_index == 3)


def keeps_even():
    return lax.rem(lax.axis_index("col"), 2) == lax.rem(lax.axis_index("row"), 2)


def early_kernel(past, own, edge1, edge2, middle2, early, away):
    got = spread(past[...], own[...], jnp.where(at_end(), edge2[...], middle2[...]), edge1[...])
    for i in range(3):
        early[i] = got[i]
    away[...] = jnp.where(keeps_even(), got[2], got[0])


def late_kernel(past, early, came, edge3, middle3, away, keep, total):
    even = keeps_even()
    (three,) = spread(past[...], jnp.where(at_end(), edge3[...], middle3[...]))
    away[...] = jnp.where(even, three, early[1])
    keep[...] = jnp.where(even, early[1], three)
    total[...] = jnp.where(even, early[0], early[2]) + came[...]


def sum_kernel(keep, came, total, own, other_low, other_top):
    near = lax.div(lax.axis_index("row"), 2) == lax.div(lax.axis_index("col"), 2)
    late = keep[...] + came[...]
    own[...] = jnp.where(near, total[...], late)
    other = jnp.where(near, late, total[...])
    other_low[...] = other[LOW, :]
    other_top[...] = other[TOP, :]


def first_kernel(side, one, two, factor, low):
    low[...] = side[LOW, :] - (one[LOW, :] + two[...])

    @pl.when(lax.axis_index("row") == 0)
    def _():
        low[...] = product(factor[LOW, columns(0)], wide(low[...]))


def top_kernel(side, one, two, factor, low, top, base):
    row_index = lax.axis_index("row")
    top[...] = side[TOP, :] - (one[TOP, :] + two[...])

    @pl.when(row_index == 1)
    def _():
        base[...] = product(factor[LOW, columns(1)], wide(low[...]))

    @pl.when(lax.axis_index("row") == 0)
    def _():
        top[...] = top[...] - product(factor[TOP, columns(0)], wide(low[...]))


def joint_kernel(factor, joint):
    @pl.when(lax.axis_index("row") == 1)
    def _():
        joint[...] = square(factor[LOW, columns(1)], factor[LOW, columns(0)])


def second_kernel(solved, base, joint, low):
    @pl.when(lax.axis_index("row") == 1)
    def _():
        low[...] = base[...] - product(joint[...], wide(solved[...]))


def five_kernel(zero, one, top_in, factor, top):
    @pl.when(lax.axis_index("row") == 1)
    def _():
        value = top_in[...] - product(factor[TOP, columns(0)], wide(zero[...]))
        top[...] = value - product(factor[TOP, columns(1)], wide(one[...]))


def last_kernel(block4, block5, last3, last7, low, low1, low2, top2, out):
    row_index = lax.axis_index("row")

    @pl.when(row_index == 0)
    def _():
        out[LOW, :] = low[...]
        out[TOP, :] = block4[...]

    @pl.when(row_index == 1)
    def _():
        out[LOW, :] = low1[...]
        out[TOP, :] = block5[...]

    @pl.when(row_index == 2)
    def _():
        out[LOW, :] = low2[...]
        out[TOP, :] = top2[...]

    @pl.when(row_index == 3)
    def _():
        out[LOW, :] = last3[...]
        out[TOP, :] = last7[...]


def halves():
    core = lax.axis_index("col") % 2
    own = pl.ds(pl.multiple_of(core * HALF, HALF), HALF)
    other = pl.ds(pl.multiple_of((1 - core) * HALF, HALF), HALF)
    return own, other


def stacked(ref, j):
    return jnp.concatenate([ref[j * BLOCK : j * BLOCK + HALF, :], ref[j * BLOCK + HALF : (j + 1) * BLOCK, :]], 1)


def join_kernel(*refs):
    out, at = refs[-1], 0
    for ref in refs[:-1]:
        out[at : at + ref.shape[0], :] = ref[...]
        at += ref.shape[0]


def zero_kernel(zero, first, low2, top2, factor, mine, theirs, state2, state3, state6, change7, joint, tile):
    @pl.when(lax.axis_index("row") == 2)
    def _():
        own, other = halves()
        pair = wide(zero[...])
        state2[...] = low2[...] - product(factor[LOW, columns(0)], pair)
        state6[...] = top2[...] - product(factor[TOP, columns(0)], pair)
        for rows, tiles in ((own, mine), (other, theirs)):
            state3[rows, :] = first[rows, :] - product(stacked(tiles, 0), pair)
            change7[rows, :] = product(stacked(tiles, 4), pair)
        sides = ((own, mine), (other, theirs))
        for rows, tiles in sides:
            tile[0, rows, :] = stacked(tiles, 13)
        for rows, tiles in sides:
            tile[1, rows, :] = square(stacked(tiles, 16), tile[0])
        for rows, tiles in sides:
            joint[rows, :] = square(stacked(tiles, 17), tile[1])


def third_kernel(
    second, state2, state3, state6, state7, factor, mine, theirs,
    block2, block3, change4, change5, value6, change7, value,
):
    @pl.when(lax.axis_index("row") == 2)
    def _():
        own, other = halves()
        sides = ((own, mine), (other, theirs))
        pairs = {1: wide(second[...])}
        block2[...] = product(
            factor[LOW, columns(2)], wide(state2[...] - product(factor[LOW, columns(1)], pairs[1]))
        )
        pairs[2] = wide(block2[...])
        for rows, tiles in sides:
            start = state3[rows, :] - product(stacked(tiles, 1), pairs[1])
            value[rows, :] = start - product(stacked(tiles, 2), pairs[2])
        pair = wide(value[...])
        for rows, tiles in sides:
            block3[rows, :] = product(stacked(tiles, 3), pair)
        pairs[3] = wide(block3[...])
        for rows, tiles in sides:
            change4[rows, :] = sum(product(stacked(tiles, 10 + k - 1), pairs[k]) for k in range(1, 4))
            change5[rows, :] = sum(product(stacked(tiles, 14 + k - 2), pairs[k]) for k in range(2, 4))
            change7[rows, :] = state7[rows, :] + sum(product(stacked(tiles, 4 + k), pairs[k]) for k in range(1, 4))
        value6[...] = state6[...] - sum(product(factor[TOP, columns(k)], pairs[k]) for k in range(1, 4))


def fourth_kernel(
    change4, change5, value6, change7, factor, mine, theirs, joint, value5, value4, top3, kept, block4, block5, sent
):
    @pl.when(lax.axis_index("row") == 2)
    def _():
        own, other = halves()
        sides = ((own, mine), (other, theirs))
        pair4 = wide(value4[...] - change4[...])
        pair5 = wide(value5[...] - change5[...])
        for rows, tiles in sides:
            block4[rows, :] = product(stacked(tiles, 13), pair4)
            block5[rows, :] = product(stacked(tiles, 17), pair5) - product(joint[rows, :], pair4)
        four, five = wide(block4[...]), wide(block5[...])
        kept[...] = value6[...] - product(factor[TOP, columns(4)], four) - product(factor[TOP, columns(5)], five)
        for rows, tiles in sides:
            start = top3[rows, :] - change7[rows, :] - product(stacked(tiles, 8), four)
            sent[rows, :] = start - product(stacked(tiles, 9), five)


def line4(right_side, prev_factor, prev_solution, window_factor):
    def move(x, *pairs):
        return lax.ppermute(x, "row", list(pairs))

    def swap(x):
        return lax.ppermute(x, "col", [(0, 1), (1, 0), (2, 3), (3, 2)])

    def cross(x):
        return lax.ppermute(x, "col", [(0, 2), (2, 0), (1, 3), (3, 1)])

    def edges(x):
        return move(x, (0, 1), (1, 0), (2, 3), (3, 2))

    def middle(x):
        return move(x, (1, 2), (2, 1))

    size, rows, tall = (BLOCK, WIDTH), (2 * BLOCK, WIDTH), prev_solution.shape
    dma = pltpu.SemaphoreType.DMA

    edge1 = edges(prev_solution)
    middle3 = middle(prev_solution)
    (carried,) = call(inject_kernel, [tall], [dma((8,))], [pltpu.VMEM, pltpu.HBM], aliases={0: 0})(
        middle3, window_factor
    )
    edge2 = edges(carried)
    middle2 = middle(edge1)
    past, factor, side, send5, send7, send8 = call(
        load_kernel,
        [prev_factor.shape, window_factor.shape, rows, tall, tall, rows],
        [dma((23,))],
        pltpu.HBM,
    )(after(prev_factor, carried, edge1), window_factor, right_side)
    (carried,) = call(inject_seven_kernel, [tall], aliases={0: 0})(middle2, send7)
    middle2 = carried
    edge3 = edges(carried)

    early, away = call(early_kernel, [(3, *rows), rows])(past, prev_solution, edge1, edge2, middle2)
    (send45,) = call(join_kernel, [(2 * tall[0], WIDTH)])(edge2, send5)
    mine45 = move(send45, (1, 2))
    tile = (BLOCK, BLOCK)
    (joint1,) = call(joint_kernel, [tile])(after(factor, early))
    away, keep, total = call(late_kernel, [rows] * 3)(past, after(early, joint1), swap(away), edge3, middle3)
    one, other_low, other_top = call(sum_kernel, [rows, size, size])(keep, swap(away), total)
    two_low, two_top = cross(other_low), cross(other_top)
    own8 = move(after(send8, one), (3, 2))
    (low,) = call(first_kernel, [size])(side, one, two_low, factor)
    first = move(low, (0, 1), (3, 2))
    zero = move(low, (0, 2))
    top, base = call(top_kernel, [size] * 2)(side, one, two_top, factor, low)
    value4 = move(top, (0, 2))
    top3 = move(top, (3, 2))
    (mine,) = call(join_kernel, [(4 * tall[0] + rows[0], WIDTH)])(edge2, edge3, own8, after(mine45, first, zero, top))
    theirs = swap(mine)
    (low1,) = call(second_kernel, [size])(first, base, joint1)
    second = move(low1, (1, 2))
    (top1,) = call(five_kernel, [size])(first, low1, top, factor)
    value5 = move(top1, (1, 2))
    *states, joint5 = call(zero_kernel, [size] * 4 + [tile], [pltpu.VMEM((2, *tile), jnp.float32)])(zero, first, low, top, factor, mine, theirs)
    block2, block3, change4, change5, value6, change7 = call(third_kernel, [size] * 6, [pltpu.VMEM(size, jnp.float32)])(
        second, *states, factor, mine, theirs
    )
    last3 = move(block3, (2, 3))
    kept, block4, block5, sent = call(fourth_kernel, [size] * 4)(
        change4, change5, value6, change7, factor, mine, theirs, joint5, value5, value4, top3
    )
    last7 = move(sent, (2, 3))
    block5 = move(block5, (2, 1))
    block4 = move(block4, (2, 0))
    return call(last_kernel, [rows], inside=False)(
        block4, block5, last3, last7, low, low1, block2, kept
    )[0]


def body(right_side, prev_factor, prev_solution, window_factor):
    blocks = window_factor.shape[1] // STEPS
    slots = right_side.shape[0] // blocks
    if lax.axis_size("row") == 4 and lax.axis_size("col") == 4 and slots == 2:
        return line4(right_side, prev_factor, prev_solution, window_factor)
    return general(right_side, prev_factor, prev_solution, window_factor)


def solution(mesh):
    in_specs = (
        P(("groups", "row"), None),
        P(("groups", "row"), "col"),
        P(("groups", "col"), "row"),
        P(("groups", "row"), None),
    )
    out_specs = P(("groups", "row"), "col")
    return jax.shard_map(body, mesh=mesh, in_specs=in_specs, out_specs=out_specs, check_vma=False)
```

```python
import jax
import jax.numpy as jnp
from jax import lax
from jax.experimental import pallas as pl
from jax.experimental.pallas import tpu as pltpu
from jax.sharding import PartitionSpec as P

NRHS = 512
STEPS = 6
HIGH = lax.Precision.HIGH


def mul(a, b):
    return jnp.dot(a, b, precision=HIGH, preferred_element_type=jnp.float32)


def general(right_side, prev_factor, prev_solution, window_factor):
    row_count = lax.axis_size("row")
    row_index = lax.axis_index("row")
    col_count = lax.axis_size("col")
    col_index = lax.axis_index("col")
    blocks = window_factor.shape[1] // STEPS
    slots = right_side.shape[0] // blocks
    width = NRHS // col_count
    partial_value = mul(prev_factor, lax.all_gather(prev_solution, "row", axis=1, tiled=True))
    prior = lax.psum_scatter(partial_value, "col", scatter_dimension=1, tiled=True)
    mine = lax.dynamic_slice_in_dim(right_side, col_index * width, width, 1)
    resid = (mine - prior).reshape(slots, blocks, width)
    tiles = window_factor.reshape(slots, blocks, STEPS, blocks)
    order = jnp.arange(slots, dtype=jnp.int32) * row_count + row_index
    for step in range(STEPS):
        root = step % row_count
        solved = mul(tiles[step // row_count, :, step, :], resid[step // row_count])
        solved = lax.psum(jnp.where(row_index == root, solved, jnp.zeros_like(solved)), "row")
        update = jnp.einsum("sij,jn->sin", tiles[:, :, step, :], solved, precision=HIGH)
        resid = jnp.where((order > step)[:, None, None], resid - update, resid)
        resid = jnp.where((order == step)[:, None, None], solved[None], resid)
    return resid.reshape(slots * blocks, width)


BLOCK = 256
HALF = BLOCK // 2
WIDTH = 128
VMEM_SPEC = pl.BlockSpec(memory_space=pltpu.VMEM)


def after(x, *earlier):
    return lax.optimization_barrier((x, *earlier))[0]


def split(x):
    high = x.astype(jnp.bfloat16)
    return high, (x - high.astype(jnp.float32)).astype(jnp.bfloat16)


def wide(x):
    return jnp.concatenate(split(x), 1)


def product(tile, pair):
    high, low = split(tile)
    both = jnp.dot(high, pair, preferred_element_type=jnp.float32)
    both = both + jnp.dot(low, pair, preferred_element_type=jnp.float32)
    return both[:, :WIDTH] + both[:, WIDTH:]


def square(one, two):
    high, low = split(one)
    pair = wide(two)
    both = jnp.dot(high, pair, preferred_element_type=jnp.float32)
    both = both + jnp.dot(low, pair, preferred_element_type=jnp.float32)
    return both[:, :BLOCK] + both[:, BLOCK:]


def columns(k):
    return slice(k * BLOCK, (k + 1) * BLOCK)


LOW, TOP = slice(0, BLOCK), slice(BLOCK, 2 * BLOCK)


def call(kernel, shapes, scratch=(), space=pltpu.VMEM, inside=True, aliases={}):
    def run(*args):
        spaces = space if isinstance(space, list) else [space] * len(args)
        return pl.pallas_call(
            kernel,
            out_shape=[(pltpu.VMEM if inside else jax.ShapeDtypeStruct)(s, jnp.float32) for s in shapes],
            in_specs=[pl.BlockSpec(memory_space=m) for m in spaces],
            out_specs=[VMEM_SPEC] * len(shapes),
            scratch_shapes=list(scratch),
            input_output_aliases=aliases,
            compiler_params=pltpu.CompilerParams(vmem_limit_bytes=32 * 1024 * 1024),
        )(*[pltpu.with_memory_space_constraint(a, m) for a, m in zip(args, spaces)])

    return run


def sent_rows():
    core = lax.axis_index("col") % 2
    low = pl.ds(pl.multiple_of(core * HALF, HALF), HALF)
    return low, pl.ds(pl.multiple_of(BLOCK + core * HALF, HALF), HALF)


def copy_all(pairs, sem):
    copies = [pltpu.make_async_copy(s, d, sem.at[i]) for i, (s, d) in enumerate(pairs)]
    for copy in copies:
        copy.start()
    for copy in copies:
        copy.wait()


def stack_copies(source, rows, start, out, count=8):
    return [
        (source.at[rows, pl.ds(start + j * HALF, HALF)], out.at[slice(j * HALF, (j + 1) * HALF), :])
        for j in range(count)
    ]


def inject_kernel(x_in, factor, x, sem):
    low, top = sent_rows()

    @pl.when(lax.axis_index("row") == 0)
    def _():
        copy_all(stack_copies(factor, top, BLOCK, x), sem)

    @pl.when(lax.axis_index("row") == 3)
    def _():
        copy_all(stack_copies(factor, low, 0, x), sem)


def inject_seven_kernel(x_in, seven, x):
    @pl.when(lax.axis_index("row") == 3)
    def _():
        x[...] = seven[...]


def load_kernel(past, factor, side, past_out, factor_out, side_out, five, seven, eight, sem):
    _, top = sent_rows()
    mine = pl.ds(pl.multiple_of(lax.axis_index("col") * WIDTH, WIDTH), WIDTH)
    copy_all(
        stack_copies(factor, top, 0, seven)
        + [
            (past, past_out),
            (factor, factor_out),
            (side.at[:, mine], side_out),
        ]
        + stack_copies(factor, top, 2 * BLOCK, five)
        + stack_copies(factor, top, 4 * BLOCK, eight, 4),
        sem,
    )


def spread(factor, *parts):
    high, low = split(factor)
    pair = jnp.concatenate([wide(x) for x in parts], 1)
    both = jnp.dot(high, pair, preferred_element_type=jnp.float32)
    both = both + jnp.dot(low, pair, preferred_element_type=jnp.float32)
    lanes = [both[:, i * WIDTH : (i + 1) * WIDTH] for i in range(2 * len(parts))]
    return [lanes[2 * i] + lanes[2 * i + 1] for i in range(len(parts))]


def at_end():
    row_index = lax.axis_index("row")
    return jnp.logical_or(row_index == 0, row_index == 3)


def keeps_even():
    return lax.rem(lax.axis_index("col"), 2) == lax.rem(lax.axis_index("row"), 2)


def early_kernel(past, own, edge1, edge2, middle2, early, away):
    got = spread(past[...], own[...], jnp.where(at_end(), edge2[...], middle2[...]), edge1[...])
    for i in range(3):
        early[i] = got[i]
    away[...] = jnp.where(keeps_even(), got[2], got[0])


def late_kernel(past, early, came, edge3, middle3, away, keep, total):
    even = keeps_even()
    (three,) = spread(past[...], jnp.where(at_end(), edge3[...], middle3[...]))
    away[...] = jnp.where(even, three, early[1])
    keep[...] = jnp.where(even, early[1], three)
    total[...] = jnp.where(even, early[0], early[2]) + came[...]


def sum_kernel(keep, came, total, own, other_low, other_top):
    near = lax.div(lax.axis_index("row"), 2) == lax.div(lax.axis_index("col"), 2)
    late = keep[...] + came[...]
    own[...] = jnp.where(near, total[...], late)
    other = jnp.where(near, late, total[...])
    other_low[...] = other[LOW, :]
    other_top[...] = other[TOP, :]


def first_kernel(side, one, two, factor, low):
    low[...] = side[LOW, :] - (one[LOW, :] + two[...])

    @pl.when(lax.axis_index("row") == 0)
    def _():
        low[...] = product(factor[LOW, columns(0)], wide(low[...]))


def top_kernel(side, one, two, factor, low, top, base):
    row_index = lax.axis_index("row")
    top[...] = side[TOP, :] - (one[TOP, :] + two[...])

    @pl.when(row_index == 1)
    def _():
        base[...] = product(factor[LOW, columns(1)], wide(low[...]))

    @pl.when(lax.axis_index("row") == 0)
    def _():
        top[...] = top[...] - product(factor[TOP, columns(0)], wide(low[...]))


def joint_kernel(factor, joint):
    @pl.when(lax.axis_index("row") == 1)
    def _():
        joint[...] = square(factor[LOW, columns(1)], factor[LOW, columns(0)])


def second_kernel(solved, base, joint, low):
    @pl.when(lax.axis_index("row") == 1)
    def _():
        low[...] = base[...] - product(joint[...], wide(solved[...]))


def five_kernel(zero, one, top_in, factor, top):
    @pl.when(lax.axis_index("row") == 1)
    def _():
        value = top_in[...] - product(factor[TOP, columns(0)], wide(zero[...]))
        top[...] = value - product(factor[TOP, columns(1)], wide(one[...]))


def last_kernel(block4, block5, last3, last7, low, low1, low2, top2, out):
    row_index = lax.axis_index("row")

    @pl.when(row_index == 0)
    def _():
        out[LOW, :] = low[...]
        out[TOP, :] = block4[...]

    @pl.when(row_index == 1)
    def _():
        out[LOW, :] = low1[...]
        out[TOP, :] = block5[...]

    @pl.when(row_index == 2)
    def _():
        out[LOW, :] = low2[...]
        out[TOP, :] = top2[...]

    @pl.when(row_index == 3)
    def _():
        out[LOW, :] = last3[...]
        out[TOP, :] = last7[...]


def halves():
    core = lax.axis_index("col") % 2
    own = pl.ds(pl.multiple_of(core * HALF, HALF), HALF)
    other = pl.ds(pl.multiple_of((1 - core) * HALF, HALF), HALF)
    return own, other


def stacked(ref, j):
    return jnp.concatenate([ref[j * BLOCK : j * BLOCK + HALF, :], ref[j * BLOCK + HALF : (j + 1) * BLOCK, :]], 1)


def join_kernel(*refs):
    out, at = refs[-1], 0
    for ref in refs[:-1]:
        out[at : at + ref.shape[0], :] = ref[...]
        at += ref.shape[0]


def zero_kernel(zero, first, low2, top2, factor, mine, theirs, state2, state3, state6, change7, joint, tile):
    @pl.when(lax.axis_index("row") == 2)
    def _():
        own, other = halves()
        pair = wide(zero[...])
        state2[...] = low2[...] - product(factor[LOW, columns(0)], pair)
        state6[...] = top2[...] - product(factor[TOP, columns(0)], pair)
        for rows, tiles in ((own, mine), (other, theirs)):
            state3[rows, :] = first[rows, :] - product(stacked(tiles, 0), pair)
            change7[rows, :] = product(stacked(tiles, 4), pair)
        sides = ((own, mine), (other, theirs))
        for rows, tiles in sides:
            tile[0, rows, :] = stacked(tiles, 13)
        for rows, tiles in sides:
            tile[1, rows, :] = square(stacked(tiles, 16), tile[0])
        for rows, tiles in sides:
            joint[rows, :] = square(stacked(tiles, 17), tile[1])


def third_kernel(
    second, state2, state3, state6, state7, factor, mine, theirs,
    block2, block3, change4, change5, value6, change7, value,
):
    @pl.when(lax.axis_index("row") == 2)
    def _():
        own, other = halves()
        sides = ((own, mine), (other, theirs))
        pairs = {1: wide(second[...])}
        block2[...] = product(
            factor[LOW, columns(2)], wide(state2[...] - product(factor[LOW, columns(1)], pairs[1]))
        )
        pairs[2] = wide(block2[...])
        for rows, tiles in sides:
            start = state3[rows, :] - product(stacked(tiles, 1), pairs[1])
            value[rows, :] = start - product(stacked(tiles, 2), pairs[2])
        pair = wide(value[...])
        for rows, tiles in sides:
            block3[rows, :] = product(stacked(tiles, 3), pair)
        pairs[3] = wide(block3[...])
        for rows, tiles in sides:
            change4[rows, :] = sum(product(stacked(tiles, 10 + k - 1), pairs[k]) for k in range(1, 4))
            change5[rows, :] = sum(product(stacked(tiles, 14 + k - 2), pairs[k]) for k in range(2, 4))
            change7[rows, :] = state7[rows, :] + sum(product(stacked(tiles, 4 + k), pairs[k]) for k in range(1, 4))
        value6[...] = state6[...] - sum(product(factor[TOP, columns(k)], pairs[k]) for k in range(1, 4))


def fourth_kernel(change4, change5, mine, theirs, joint, value5, value4, block4, block5):
    @pl.when(lax.axis_index("row") == 2)
    def _():
        own, other = halves()
        pair4 = wide(value4[...] - change4[...])
        pair5 = wide(value5[...] - change5[...])
        for rows, tiles in ((own, mine), (other, theirs)):
            block4[rows, :] = product(stacked(tiles, 13), pair4)
            block5[rows, :] = product(stacked(tiles, 17), pair5) - product(joint[rows, :], pair4)


def fifth_kernel(block4, block5, value6, change7, factor, mine, theirs, top3, kept, sent):
    @pl.when(lax.axis_index("row") == 2)
    def _():
        own, other = halves()
        four, five = wide(block4[...]), wide(block5[...])
        kept[...] = value6[...] - product(factor[TOP, columns(4)], four) - product(factor[TOP, columns(5)], five)
        for rows, tiles in ((own, mine), (other, theirs)):
            start = top3[rows, :] - change7[rows, :] - product(stacked(tiles, 8), four)
            sent[rows, :] = start - product(stacked(tiles, 9), five)


def line4(right_side, prev_factor, prev_solution, window_factor):
    def move(x, *pairs):
        return lax.ppermute(x, "row", list(pairs))

    def swap(x):
        return lax.ppermute(x, "col", [(0, 1), (1, 0), (2, 3), (3, 2)])

    def cross(x):
        return lax.ppermute(x, "col", [(0, 2), (2, 0), (1, 3), (3, 1)])

    def edges(x):
        return move(x, (0, 1), (1, 0), (2, 3), (3, 2))

    def middle(x):
        return move(x, (1, 2), (2, 1))

    size, rows, tall = (BLOCK, WIDTH), (2 * BLOCK, WIDTH), prev_solution.shape
    dma = pltpu.SemaphoreType.DMA

    edge1 = edges(prev_solution)
    middle3 = middle(prev_solution)
    (carried,) = call(inject_kernel, [tall], [dma((8,))], [pltpu.VMEM, pltpu.HBM], aliases={0: 0})(
        middle3, window_factor
    )
    edge2 = edges(carried)
    middle2 = middle(edge1)
    past, factor, side, send5, send7, send8 = call(
        load_kernel,
        [prev_factor.shape, window_factor.shape, rows, tall, tall, rows],
        [dma((23,))],
        pltpu.HBM,
    )(after(prev_factor, carried, edge1), window_factor, right_side)
    (carried,) = call(inject_seven_kernel, [tall], aliases={0: 0})(middle2, send7)
    middle2 = carried
    edge3 = edges(carried)

    early, away = call(early_kernel, [(3, *rows), rows])(past, prev_solution, edge1, edge2, middle2)
    (send45,) = call(join_kernel, [(2 * tall[0], WIDTH)])(edge2, send5)
    mine45 = move(send45, (1, 2))
    tile = (BLOCK, BLOCK)
    (joint1,) = call(joint_kernel, [tile])(after(factor, early))
    away, keep, total = call(late_kernel, [rows] * 3)(past, after(early, joint1), swap(away), edge3, middle3)
    one, other_low, other_top = call(sum_kernel, [rows, size, size])(keep, swap(away), total)
    two_low, two_top = cross(other_low), cross(other_top)
    own8 = move(after(send8, one), (3, 2))
    (low,) = call(first_kernel, [size])(side, one, two_low, factor)
    first = move(low, (0, 1), (3, 2))
    zero = move(low, (0, 2))
    top, base = call(top_kernel, [size] * 2)(side, one, two_top, factor, low)
    value4 = move(top, (0, 2))
    top3 = move(top, (3, 2))
    (mine,) = call(join_kernel, [(4 * tall[0] + rows[0], WIDTH)])(edge2, edge3, own8, after(mine45, first, zero, top))
    theirs = swap(mine)
    (low1,) = call(second_kernel, [size])(first, base, joint1)
    second = move(low1, (1, 2))
    (top1,) = call(five_kernel, [size])(first, low1, top, factor)
    value5 = move(top1, (1, 2))
    *states, joint5 = call(zero_kernel, [size] * 4 + [tile], [pltpu.VMEM((2, *tile), jnp.float32)])(zero, first, low, top, factor, mine, theirs)
    block2, block3, change4, change5, value6, change7 = call(third_kernel, [size] * 6, [pltpu.VMEM(size, jnp.float32)])(
        second, *states, factor, mine, theirs
    )
    last3 = move(block3, (2, 3))
    block4, block5 = call(fourth_kernel, [size] * 2)(change4, change5, mine, theirs, joint5, value5, value4)
    kept, sent = call(fifth_kernel, [size] * 2)(block4, block5, value6, change7, factor, mine, theirs, top3)
    last7 = move(sent, (2, 3))
    block5 = move(block5, (2, 1))
    block4 = move(block4, (2, 0))
    return call(last_kernel, [rows], inside=False)(
        block4, block5, last3, last7, low, low1, block2, kept
    )[0]


def body(right_side, prev_factor, prev_solution, window_factor):
    blocks = window_factor.shape[1] // STEPS
    slots = right_side.shape[0] // blocks
    if lax.axis_size("row") == 4 and lax.axis_size("col") == 4 and slots == 2:
        return line4(right_side, prev_factor, prev_solution, window_factor)
    return general(right_side, prev_factor, prev_solution, window_factor)


def solution(mesh):
    in_specs = (
        P(("groups", "row"), None),
        P(("groups", "row"), "col"),
        P(("groups", "col"), "row"),
        P(("groups", "row"), None),
    )
    out_specs = P(("groups", "row"), "col")
    return jax.shard_map(body, mesh=mesh, in_specs=in_specs, out_specs=out_specs, check_vma=False)
```
